256 devices in a mesh: dp: 16 (over z_hi, y), fsdp: 16 (over x, z_lo, core).
Axes of the slice: x: 4, y: 4, z: 8 (z_hi: 4, z_lo: 2; z = z_hi * 2 + z_lo), core: 2. Of those that a mesh axis runs over, the one named last changes fastest.
Arguments:
- tokens: bfloat16 [32768, 4096], P(('dp', 'fsdp')), may hold values from -6 to 6
- route_ids: int32 [32768, 4], P(('dp', 'fsdp')), may hold values from 0 to 15, all different within a row; in each aligned block of 128 rows (0 to 127, 128 to 255, ...) at most 48 rows name the same one
- gate_values: float32 [32768, 4], P(('dp', 'fsdp')), may hold values from 0.1 to 1
- w_gate_up: bfloat16 [16, 4096, 1536], P('dp', 'fsdp'), may hold values from -0.09375 to 0.09375
- w_down: bfloat16 [16, 768, 4096], P('dp', None, 'fsdp'), may hold values from -0.21875 to 0.21875
Outputs:
- combined: bfloat16 [32768, 4096], P(('dp', 'fsdp'))
The draws below stay inside these ranges and needn't reach their ends.
Inputs may be any that keep to these rules, and one draw needn't show every extreme that they name: `route_ids`: each row names 4 different experts. Among the rows of one device no expert is named by more than 48 rows, a bound that some block reaches of some device in every draw.
All inputs are finite; a program needn't handle non-finite values.
Results may differ from the reference program's by a relative error of at most 0.0058.
Values may be sent and summed in bfloat16 or wider, within the bound.
No kernel may reach another device: no remote copies, remote signals or barrier semaphores. Data moves between devices by JAX's collectives and lax.ppermute only.
A program may use at most 128 MiB of HBM per device.

```python
import math
import jax
import jax.numpy as jnp
import numpy as np
from jax import lax

D = 4096
FF = 768
TOP = 4
TOK_DEV = 128
EXPERTS = 16
CAP = 48
TOKENS = 32768


def levels(key, dims, cuts, smallest, high):
    loudness, own = 1.0, jax.random.fold_in(key, 6)
    for dim, blocks in cuts:
        draws = jnp.exp(jax.random.uniform(jax.random.fold_in(own, dim), (blocks,), jnp.float32, smallest / len(cuts), high / len(cuts)))
        loudness = loudness * jnp.repeat(draws, dims[dim] // blocks).reshape([-1 if axis == dim else 1 for axis in range(len(dims))])
    return loudness


def routed_block(stream_key, own, number, rows, number_of, top, limit, skew):
    ranking = jax.random.permutation(stream_key, number_of)
    crowded, ordinary = portions_of(number_of, rows * top, limit, skew, True), portions_of(number_of, rows * top, limit, skew, False)
    places = jnp.arange(number_of)

    def named(lengths, turn):
        used = int((lengths > 0).sum())
        fixed = max(1, used // 4)
        shifted = fixed + (places - fixed + turn * (used - fixed)) % max(1, number_of - fixed)
        return jnp.zeros((number_of,), jnp.int32).at[ranking[jnp.where(places < fixed, places, shifted)]].set(jnp.asarray(lengths, jnp.int32))

    lengths = jnp.where(number % 4 == 0, named(crowded, number // 4), named(ordinary, number - number // 4 - 1))
    mixed = jax.random.permutation(jax.random.fold_in(own, 3), number_of)
    source_of, taker = mixed[0:number_of // 2 * 2:2], mixed[1:number_of // 2 * 2:2]
    room = jnp.minimum(lengths[source_of] - 1, limit - lengths[taker]) // 2
    room = jnp.where((source_of == ranking[0]) | (taker == ranking[0]) | (lengths[taker] == 0), 0, jnp.maximum(room, 0))
    shifted = jax.random.randint(jax.random.fold_in(own, 4), (number_of // 2,), 0, 1 << 20) % (room + 1)
    lengths = lengths.at[source_of].add(-shifted).at[taker].add(shifted)
    members = jnp.searchsorted(jnp.cumsum(lengths), jnp.arange(rows * top), side="right").astype(jnp.int32)
    listing = members.reshape(top, rows).T
    listing = listing[jax.random.permutation(jax.random.fold_in(own, 1), rows)]
    turn = jax.random.randint(jax.random.fold_in(own, 2), (rows, 1), 0, top)
    return jnp.take_along_axis(listing, (jnp.arange(top)[None, :] + turn) % top, axis=1)


def portions_of(number_of, total, bound, slope, full):
    loads = [(1 << 20) // math.isqrt(grade ** slope) + 1 for grade in range(1, number_of + 1)]
    largest = bound if full else min(bound, max(-(-total // number_of), total * loads[0] // sum(loads)))
    least = 1 if total - largest >= number_of - 1 else 0
    given, rest = [largest] + [least] * (number_of - 1), total - largest - least * (number_of - 1)
    while rest > 0:
        free = [i for i in range(1, number_of) if given[i] < largest] or [i for i in range(1, number_of) if given[i] < bound]
        mass, budget = sum([loads[i] for i in free]), rest
        for i in free:
            extra = min(bound - given[i], max(1, budget * loads[i] // mass), rest)
            given[i] = given[i] + extra
            rest = rest - extra
    return np.array(given)


def centred(rng, extent, deviation, limit, shards=(), held_as=jnp.bfloat16):
    values = jax.random.normal(rng, extent, jnp.float32) * deviation
    if len(shards) > 0:
        values = levels(rng, extent, shards, -0.22, 0.18) * values
    return jnp.clip(values, min=-limit, max=limit).astype(held_as)


def setup_inputs(seed: int = 0) -> dict:
    arg_keys = jax.random.split(jax.random.key(seed), 6)
    tokens = centred(arg_keys[0], (TOKENS, D), 1.0, 6.0, ((0, 256),))
    route_ids_keys = jax.random.split(jax.random.fold_in(arg_keys[1], 1), TOKENS // TOK_DEV)
    route_ids_turns = jax.random.permutation(jax.random.fold_in(arg_keys[1], 3), TOKENS // TOK_DEV)
    route_ids = jax.vmap(lambda own, number: routed_block(jax.random.fold_in(arg_keys[1], 2), own, number, TOK_DEV, EXPERTS, TOP, CAP, 2))(route_ids_keys, route_ids_turns).reshape((TOKENS, TOP))
    gate_values = jnp.clip(jnp.exp(math.log(1.0) - 2.3025851 * jax.random.uniform(arg_keys[2], (TOKENS, TOP), jnp.float32) ** levels(arg_keys[2], (TOKENS, TOP), ((0, 256),), -0.2, 0.2)), 0.1, 1.0)
    w_gate_up = centred(arg_keys[3], (EXPERTS, D, 2 * FF), D ** -0.5, 0.09375, ((0, 16), (1, 16)))
    w_down = centred(arg_keys[4], (EXPERTS, FF, D), FF ** -0.5, 0.21875, ((0, 16), (2, 16)))
    return dict(tokens=tokens, route_ids=route_ids, gate_values=gate_values, w_gate_up=w_gate_up, w_down=w_down)


def reference(tokens, route_ids, gate_values, w_gate_up, w_down):
    blocks = TOKENS // TOK_DEV
    routes_per = TOK_DEV * TOP
    grouped = route_ids.reshape(blocks, routes_per)
    weights_flat = gate_values.reshape(blocks, routes_per)
    block_index = jnp.arange(blocks, dtype=jnp.int32)[:, None]
    owner = block_index * TOK_DEV + jnp.arange(routes_per, dtype=jnp.int32)[None, :] // TOP
    padded = jnp.concatenate([tokens, jnp.zeros((1, D), tokens.dtype)], axis=0)

    def per_expert(totals, expert):
        matched = grouped == expert
        slot_index = jnp.where(matched, jnp.cumsum(matched.astype(jnp.int32), axis=1) - 1, CAP).astype(jnp.int32)
        source = jnp.full((blocks, CAP + 1), TOKENS, jnp.int32).at[block_index, slot_index].set(
            jnp.where(matched, owner, TOKENS).astype(jnp.int32))
        scale_table = jnp.zeros((blocks, CAP + 1), jnp.float32).at[block_index, slot_index].set(
            jnp.where(matched, weights_flat, jnp.zeros_like(weights_flat)))
        source = source[:, :CAP].reshape(-1)
        scale_table = scale_table[:, :CAP].reshape(-1)
        expert_rows = padded[source].astype(jnp.float32)
        up_weight = lax.dynamic_index_in_dim(w_gate_up, expert, 0, keepdims=False).astype(jnp.float32)
        down_weight = lax.dynamic_index_in_dim(w_down, expert, 0, keepdims=False).astype(jnp.float32)
        projected = jnp.dot(expert_rows, up_weight, precision=lax.Precision.HIGHEST)
        hidden = (jax.nn.silu(projected[:, :FF]) * projected[:, FF:]).astype(jnp.bfloat16)
        hidden = lax.optimization_barrier(hidden)
        produced = jnp.dot(hidden.astype(jnp.float32), down_weight, precision=lax.Precision.HIGHEST).astype(jnp.bfloat16)
        produced = lax.optimization_barrier(produced)
        totals = totals.at[source].add(scale_table[:, None] * produced.astype(jnp.float32), mode="drop")
        return totals, None

    totals, unused = lax.scan(per_expert, jnp.zeros((TOKENS, D), jnp.float32), jnp.arange(EXPERTS, dtype=jnp.int32))
    return totals.astype(jnp.bfloat16)
```

```python
import jax
import jax.numpy as jnp
from jax import lax
from jax.experimental import pallas as pl
from jax.experimental.pallas import tpu as pltpu
from jax.sharding import Mesh, PartitionSpec as P

BF, F32 = jnp.bfloat16, jnp.float32
ZH, YS = 4, 4
CHUNKS = 4
PARAMS = pltpu.CompilerParams(vmem_limit_bytes=48 << 20)


def ring(step):
    return [(i, (i + step) % ZH) for i in range(ZH)]


def plan_kernel(group_ref, *refs):
    metas, (pick_ref, high_ref, low_ref) = refs[:ZH], refs[ZH:]
    rows = metas[0].shape[1]
    slots = pick_ref.shape[1] // YS
    group = group_ref[0]
    named, gates = [], []
    for k in range(ZH):
        ids, weights = metas[k][0:4, :], metas[k][4:8, :]
        for y in range(YS):
            match = ids == (group * YS + y).astype(F32)
            named.append(jnp.sum(match.astype(F32), axis=0, keepdims=True))
            gates.append(jnp.sum(jnp.where(match, weights, 0.0), axis=0, keepdims=True))
    stacked = jnp.concatenate(named, axis=0)
    earlier = lax.broadcasted_iota(jnp.int32, (rows, rows), 0)
    later = lax.broadcasted_iota(jnp.int32, (rows, rows), 1)
    rank = jnp.dot(
        stacked.astype(BF), (earlier < later).astype(F32).astype(BF), preferred_element_type=F32
    )
    slot = lax.broadcasted_iota(jnp.int32, (slots, rows), 0).astype(F32)
    for k in range(ZH):
        for y in range(YS):
            i = k * YS + y
            here = (rank[i : i + 1, :] == slot) & (named[i] > 0.5)
            at = slice(y * slots, (y + 1) * slots)
            scaled = jnp.where(here, gates[i], 0.0)
            high = scaled.astype(BF)
            pick_ref[k, at, :] = here.astype(F32).astype(BF)
            high_ref[k, at, :] = high
            low_ref[k, at, :] = (scaled - high.astype(F32)).astype(BF)


def plan(group, metas, slots):
    rows = metas[0].shape[1]
    out = jax.ShapeDtypeStruct((ZH, YS * slots, rows), BF)
    return pl.pallas_call(
        plan_kernel,
        out_shape=(out, out, out),
        in_specs=[pl.BlockSpec(memory_space=pltpu.SMEM)] + [pl.BlockSpec()] * ZH,
        compiler_params=PARAMS,
        name="plan",
    )(group, *metas)


def gather_kernel(pick_ref, *refs):
    blocks, out_ref = refs[:ZH], refs[ZH]
    slots = out_ref.shape[2]
    for k in range(ZH):
        got = jnp.dot(pick_ref[k], blocks[k][...], preferred_element_type=F32).astype(BF)
        for y in range(YS):
            out_ref[y, k] = got[y * slots : (y + 1) * slots]


def gather(pick, blocks, slots):
    width = blocks[0].shape[1]
    return pl.pallas_call(
        gather_kernel,
        out_shape=jax.ShapeDtypeStruct((YS, ZH, slots, width), BF),
        compiler_params=PARAMS,
        name="gather",
    )(pick, *blocks)


def first_kernel(x_ref, wg_ref, wu_ref, *refs):
    g = jnp.dot(x_ref[...], wg_ref[...], preferred_element_type=F32)
    u = jnp.dot(x_ref[...], wu_ref[...], preferred_element_type=F32)
    n_in = len(refs) - (1 if refs[-1].dtype == BF else 2)
    if n_in:
        g, u = g + refs[0][...], u + refs[1][...]
    if refs[-1].dtype == BF:
        refs[-1][...] = (g / (1.0 + jnp.exp(-g)) * u).astype(BF)
    else:
        refs[-2][...], refs[-1][...] = g, u


def first(x, w, at, sums, last):
    rows, width = x.shape
    half = w.shape[1] // 2
    tile = 256
    steps = half // tile
    part = pl.BlockSpec((rows, tile), lambda j: (0, j))
    shape = jax.ShapeDtypeStruct((rows, half), BF if last else F32)
    return pl.pallas_call(
        first_kernel,
        grid=(steps,),
        out_shape=shape if last else (shape, shape),
        in_specs=[
            pl.BlockSpec((rows, width), lambda j: (0, 0)),
            pl.BlockSpec((width, tile), lambda j: (at, j)),
            pl.BlockSpec((width, tile), lambda j: (at, j + steps)),
        ]
        + [part] * len(sums),
        out_specs=part if last else (part, part),
        compiler_params=PARAMS,
        name="first",
    )(x, w, w, *sums)


def second_kernel(h_ref, w_ref, out_ref):
    out_ref[...] = jnp.dot(h_ref[...], w_ref[...], preferred_element_type=F32).astype(BF)


def second(hidden, w, at, width):
    rows, inner = hidden.shape
    tile = 256
    steps = width // tile
    return pl.pallas_call(
        second_kernel,
        grid=(steps,),
        out_shape=jax.ShapeDtypeStruct((rows, width), BF),
        in_specs=[
            pl.BlockSpec((rows, inner), lambda j: (0, 0)),
            pl.BlockSpec((pl.Squeezed(), inner, tile), lambda j: (at * steps + j, 0, 0)),
        ],
        out_specs=pl.BlockSpec((rows, tile), lambda j: (0, j)),
        compiler_params=PARAMS,
        name="second",
    )(hidden, w)


def combine_kernel(high_ref, low_ref, rows_ref, *outs):
    for k in range(ZH):
        rows = jnp.concatenate([rows_ref[y, k] for y in range(YS)], axis=0)
        total = sum(
            lax.dot_general(
                s[k], rows, (((0,), (0,)), ((), ())), preferred_element_type=F32
            )
            for s in (high_ref, low_ref)
        )
        outs[k][...] = total.astype(outs[k].dtype)


def combine(high, low, rows, tok_rows):
    width = rows.shape[-1]
    return pl.pallas_call(
        combine_kernel,
        out_shape=tuple(
            jax.ShapeDtypeStruct((tok_rows, width), F32 if k == 0 else BF) for k in range(ZH)
        ),
        compiler_params=PARAMS,
        name="combine",
    )(high, low, rows)


def on_device(tokens, route_ids, gate_values, w_gate_up, w_down):
    tok_rows, top = route_ids.shape
    model = tokens.shape[1]
    slots = 3 * tok_rows * top // (2 * ZH * YS)
    width = model // CHUNKS
    meta = jnp.concatenate([route_ids.astype(F32).T, gate_values.T], axis=0)
    metas = [meta] + [lax.ppermute(meta, "zh", ring(k)) for k in range(1, ZH)]
    w_in = lax.all_gather(w_gate_up[0], "fsdp", axis=0, tiled=True)
    w_out = lax.all_gather(w_down[0], "fsdp", axis=0, tiled=False)
    group = lax.axis_index("zh").reshape(1)
    pick, high, low = plan(group, metas, slots)

    sums = ()
    for c in range(CHUNKS):
        own = tokens[:, c * width : (c + 1) * width]
        blocks = [own] + [lax.ppermute(own, "zh", ring(k)) for k in range(1, ZH)]
        sent = gather(pick, blocks, slots).reshape(YS, ZH * slots, width)
        rows = lax.all_to_all(sent, "y", split_axis=0, concat_axis=0, tiled=True)
        sums = first(rows.reshape(-1, width), w_in, c, sums, c == CHUNKS - 1)
    hidden = sums

    outs = []
    for c in range(CHUNKS):
        made = second(hidden, w_out, c, width).reshape(YS, ZH * slots, width)
        back = lax.all_to_all(made, "y", split_axis=0, concat_axis=0, tiled=True)
        parts = combine(high, low, back.reshape(YS, ZH, slots, width), tok_rows)
        total = parts[0]
        for k in range(1, ZH):
            total = total + lax.ppermute(parts[k], "zh", ring(-k)).astype(F32)
        outs.append(total.astype(BF))
    return jnp.concatenate(outs, axis=1)


def solution(mesh):
    split = Mesh(mesh.devices.reshape(ZH, YS, -1), ("zh", "y", "fsdp"))
    every, owner = ("zh", "y", "fsdp"), ("zh", "y")
    in_specs = (P(every, None),) * 3 + (P(owner, "fsdp", None), P(owner, None, "fsdp"))
    return jax.shard_map(
        on_device, mesh=split, in_specs=in_specs, out_specs=P(every, None), check_vma=False
    )
```

```python
import functools

import jax
import jax.numpy as jnp
from jax import lax
from jax.experimental import pallas as pl
from jax.experimental.pallas import tpu as pltpu
from jax.sharding import Mesh, PartitionSpec as P

BF, F32 = jnp.bfloat16, jnp.float32
ZH, YS, XS = 4, 4, 4
PARAMS = pltpu.CompilerParams(vmem_limit_bytes=48 << 20)
BLOCK = 256
ANY = pl.BlockSpec(memory_space=pl.ANY)


def ring(step):
    return [(i, (i + step) % ZH) for i in range(ZH)]


def plan_kernel(group_ref, meta_ref, pick_ref, high_ref, low_ref):
    sources, _, rows = meta_ref.shape
    slots = pick_ref.shape[1] // YS
    group = group_ref[0]
    named, gates = [], []
    for k in range(sources):
        ids, weights = meta_ref[k, 0:4, :], meta_ref[k, 4:8, :]
        for y in range(YS):
            match = ids == (group * YS + y).astype(F32)
            named.append(jnp.sum(match.astype(F32), axis=0, keepdims=True))
            gates.append(jnp.sum(jnp.where(match, weights, 0.0), axis=0, keepdims=True))
    stacked = jnp.concatenate(named, axis=0)
    earlier = lax.broadcasted_iota(jnp.int32, (rows, rows), 0)
    later = lax.broadcasted_iota(jnp.int32, (rows, rows), 1)
    rank = jnp.dot(
        stacked.astype(BF), (earlier < later).astype(F32).astype(BF), preferred_element_type=F32
    )
    slot = lax.broadcasted_iota(jnp.int32, (slots, rows), 0).astype(F32)
    for k in range(sources):
        for y in range(YS):
            i = k * YS + y
            here = (rank[i : i + 1, :] == slot) & (named[i] > 0.5)
            at = slice(y * slots, (y + 1) * slots)
            scaled = jnp.where(here, gates[i], 0.0)
            high = scaled.astype(BF)
            pick_ref[k, at, :] = here.astype(F32).astype(BF)
            high_ref[k, at, :] = high
            low_ref[k, at, :] = (scaled - high.astype(F32)).astype(BF)


def plan(group, metas, slots):
    out = jax.ShapeDtypeStruct((metas.shape[0], YS * slots, metas.shape[2]), BF)
    return pl.pallas_call(
        plan_kernel,
        out_shape=(out, out, out),
        in_specs=[pl.BlockSpec(memory_space=pltpu.SMEM), pl.BlockSpec()],
        compiler_params=PARAMS,
        name="plan",
    )(group, metas)


def gather_kernel(pick_ref, *refs):
    blocks, out_ref = refs[:-1], refs[-1]
    rows = jnp.concatenate([ref[...] for ref in blocks], axis=0)
    out_ref[...] = jnp.dot(pick_ref[0], rows, preferred_element_type=F32).astype(BF)


def gather(pick, k, *blocks):
    _, routes, rows = pick.shape
    width = blocks[0].shape[1]
    tile = 1024
    return pl.pallas_call(
        gather_kernel,
        grid=(width // tile,),
        out_shape=jax.ShapeDtypeStruct((routes, width), BF),
        in_specs=[pl.BlockSpec((1, routes, rows), lambda j: (k, 0, 0))]
        + [pl.BlockSpec((b.shape[0], tile), lambda j: (0, j)) for b in blocks],
        out_specs=pl.BlockSpec((routes, tile), lambda j: (0, j)),
        compiler_params=PARAMS,
        name="gather",
    )(pick, *blocks)


def expert_kernel(place_ref, x_ref, *refs):
    ins, downs = refs[0:4], refs[4:8]
    out_ref, sums_ref, hidden_ref = refs[-3:]
    step = pl.program_id(0)
    parts = sums_ref.shape[0]
    half = parts // 2

    def columns(x, r):
        return pl.ds(pl.multiple_of((x * 4 + place_ref[r]) * BLOCK, BLOCK), BLOCK)

    @pl.when(step == 0)
    def _():
        sums_ref[...] = jnp.zeros_like(sums_ref)

    @pl.when(step < XS)
    def _():
        rows = [x_ref[:, columns(step, r)] for r in range(4)]
        for n in range(parts):
            sums_ref[n] += sum(
                jnp.dot(rows[r], ins[r][n], preferred_element_type=F32) for r in range(4)
            )

    @pl.when(step == XS)
    def _():
        for n in range(half):
            g, u = sums_ref[n], sums_ref[half + n]
            hidden_ref[n] = (g / (1.0 + jnp.exp(-g)) * u).astype(BF)

    @pl.when(step >= XS)
    def _():
        for r in range(4):
            made = sum(
                jnp.dot(hidden_ref[n], downs[r][n], preferred_element_type=F32) for n in range(half)
            )
            out_ref[:, columns(step - XS, r)] = made.astype(BF)


def expert(place, rows, packs, after):
    count, width = rows.shape
    total = packs[0].shape[1]
    half = total // 3
    return pl.pallas_call(
        expert_kernel,
        grid_spec=pltpu.PrefetchScalarGridSpec(
            num_scalar_prefetch=1,
            grid=(2 * XS,),
            in_specs=[pl.BlockSpec((count, width), lambda s, p: (0, 0))]
            + [
                pl.BlockSpec(
                    (pl.Squeezed(), 2 * half, BLOCK, BLOCK),
                    lambda s, p: (jnp.minimum(s, XS - 1), 0, 0, 0),
                )
            ]
            * 4
            + [
                pl.BlockSpec(
                    (pl.Squeezed(), half, BLOCK, BLOCK),
                    lambda s, p: (jnp.maximum(s - XS, 0), 2, 0, 0),
                )
            ]
            * 4
            + [ANY] * len(after),
            out_specs=pl.BlockSpec((count, width), lambda s, p: (0, 0)),
            scratch_shapes=[
                pltpu.VMEM((2 * half, count, BLOCK), F32),
                pltpu.VMEM((half, count, BLOCK), BF),
            ],
        ),
        out_shape=jax.ShapeDtypeStruct((count, width), BF),
        compiler_params=PARAMS,
        name="expert",
    )(place, rows, *packs, *packs, *after)


def combine_kernel(start, high_ref, low_ref, rows_ref, *refs):
    rows, out_ref = rows_ref[...], refs[-1]
    total = sum(
        lax.dot_general(s[0], rows, (((0,), (0,)), ((), ())), preferred_element_type=F32)
        for s in (high_ref, low_ref)
    )
    if len(refs) == 1:
        out_ref[...] = total.astype(out_ref.dtype)
        return
    half = refs[0].shape[0]
    for at in (0, half):
        part = total[at : at + half]
        if at == start:
            part = part + refs[0][...].astype(F32)
        out_ref[at : at + half, :] = part.astype(out_ref.dtype)


def combine(plans, k, rows, dtype, passed=(), start=0):
    _, high, low = plans
    _, routes, tok_rows = high.shape
    width = rows.shape[1]
    tile = 1024
    pick = pl.BlockSpec((1, routes, tok_rows), lambda j: (k, 0, 0))
    return pl.pallas_call(
        functools.partial(combine_kernel, start),
        grid=(width // tile,),
        out_shape=jax.ShapeDtypeStruct((tok_rows, width), dtype),
        in_specs=[pick, pick, pl.BlockSpec((routes, tile), lambda j: (0, j))]
        + [pl.BlockSpec((p.shape[0], tile), lambda j: (0, j)) for p in passed],
        out_specs=pl.BlockSpec((tok_rows, tile), lambda j: (0, j)),
        compiler_params=PARAMS,
        name="combine",
    )(high, low, rows, *passed)


def over_y(rows):
    routes, width = rows.shape
    split = rows.reshape(YS, routes // YS, width)
    return lax.all_to_all(split, "y", split_axis=0, concat_axis=0, tiled=True).reshape(rows.shape)


def on_device(tokens, route_ids, gate_values, w_gate_up, w_down):
    tok_rows, top = route_ids.shape
    slots = 3 * tok_rows * top // (2 * ZH * YS)
    parts = w_gate_up.shape[2] // BLOCK
    swap = [(0, 1), (1, 0)]
    pack = jnp.concatenate(
        [
            w_gate_up[0].reshape(BLOCK, parts, BLOCK).transpose(1, 0, 2),
            w_down[0].reshape(parts // 2, BLOCK, BLOCK),
        ],
        axis=0,
    )
    meta = jnp.concatenate([route_ids.astype(F32).T, gate_values.T], axis=0)
    group = lax.axis_index("zh").reshape(1)
    barrier = lax.optimization_barrier

    near = [lax.ppermute(tokens, "zh", ring(k)) for k in (1, 3)]
    swapped = lax.ppermute(pack, "zl", swap)
    metas = [lax.ppermute(meta, "zh", ring(k)) for k in (1, 2, 3)]
    mine = lax.all_gather(pack, "x")
    own_plan = plan(group, meta[None], slots)
    arrived = {0: over_y(gather(own_plan[0], 0, tokens))}
    near, swapped, metas, arrived[0] = barrier((near, swapped, metas, arrived[0]))
    other = lax.all_gather(swapped, "x")
    far_plan = plan(group, jnp.stack(metas), slots)

    half = tok_rows // 2
    far = [lax.ppermute(near[0][:half], "zh", ring(1)), lax.ppermute(near[1][half:], "zh", ring(3))]
    arrived[1] = over_y(gather(far_plan[0], 0, near[0]))
    far, mine, near[1], arrived[1] = barrier((far, mine, near[1], arrived[1]))
    mine_swapped = lax.ppermute(mine, "core", swap)
    arrived[3] = over_y(gather(far_plan[0], 2, near[1]))
    arrived[2] = over_y(gather(far_plan[0], 1, *far))
    other, arrived[2], arrived[3], mine_swapped = barrier((other, arrived[2], arrived[3], mine_swapped))
    packs = [mine, mine_swapped, other, lax.ppermute(other, "core", swap)]
    zl, core = lax.axis_index("zl"), lax.axis_index("core")
    place = jnp.stack([zl * 2 + core, zl * 2 + 1 - core, (1 - zl) * 2 + core, (1 - zl) * 2 + 1 - core])

    def returned(k, after):
        return over_y(expert(place, arrived[k], packs, after))

    across = combine(far_plan, 1, returned(2, []), BF)
    back = {1: returned(1, [])}
    passed = [lax.ppermute(across[:half], "zh", ring(3)), lax.ppermute(across[half:], "zh", ring(1))]
    back[3] = returned(3, [across])
    below = combine(far_plan, 0, back[1], BF, passed[:1], 0)
    back[0] = returned(0, [below])
    above = combine(far_plan, 2, back[3], BF, passed[1:], half)
    total = combine(own_plan, 0, back[0], F32)
    for part, step in ((below, 3), (above, 1)):
        total = total + lax.ppermute(part, "zh", ring(step)).astype(F32)
    return total.astype(BF)


def solution(mesh):
    split = Mesh(mesh.devices.reshape(ZH, YS, XS, 2, 2), ("zh", "y", "x", "zl", "core"))
    owner, shard = ("zh", "y"), ("x", "zl", "core")
    every = owner + shard
    in_specs = (P(every, None),) * 3 + (P(owner, shard, None), P(owner, None, shard))
    return jax.shard_map(
        on_device, mesh=split, in_specs=in_specs, out_specs=P(every, None), check_vma=False
    )
```

```python
import functools

import jax
import jax.numpy as jnp
from jax import lax
from jax.experimental import pallas as pl
from jax.experimental.pallas import tpu as pltpu
from jax.sharding import Mesh, PartitionSpec as P

BF, F32 = jnp.bfloat16, jnp.float32
ZH, YS, XS = 4, 4, 4
PARAMS = pltpu.CompilerParams(vmem_limit_bytes=56 << 20)
BLOCK = 256
TILE = 1024


def ring(step):
    return [(i, (i + step) % ZH) for i in range(ZH)]


def pack_kernel(up_ref, down_ref, out_ref):
    step = pl.program_id(0)

    @pl.when(step < 2)
    def _():
        for n in range(3):
            out_ref[n] = up_ref[:, n * BLOCK : (n + 1) * BLOCK]

    @pl.when(step == 2)
    def _():
        for n in range(3):
            out_ref[n] = down_ref[n * BLOCK : (n + 1) * BLOCK, :]


def pack_shards(up, down):
    return pl.pallas_call(
        pack_kernel,
        grid=(3,),
        out_shape=jax.ShapeDtypeStruct((9, BLOCK, BLOCK), BF),
        in_specs=[
            pl.BlockSpec((BLOCK, 3 * BLOCK), lambda s: (0, jnp.minimum(s, 1))),
            pl.BlockSpec((3 * BLOCK, BLOCK), lambda s: (0, 0)),
        ],
        out_specs=pl.BlockSpec((3, BLOCK, BLOCK), lambda s: (s, 0, 0)),
        compiler_params=PARAMS,
        name="pack",
    )(up, down)


def plan_kernel(group_ref, *refs):
    metas, (pick_ref, high_ref, low_ref) = refs[:-3], refs[-3:]
    rows = metas[0].shape[1]
    slots = pick_ref.shape[1] // YS
    group = group_ref[0]
    named, gates = [], []
    for meta_ref in metas:
        ids, weights = meta_ref[0:4, :], meta_ref[4:8, :]
        for y in range(YS):
            match = ids == (group * YS + y).astype(F32)
            named.append(jnp.sum(match.astype(F32), axis=0, keepdims=True))
            gates.append(jnp.sum(jnp.where(match, weights, 0.0), axis=0, keepdims=True))
    stacked = jnp.concatenate(named, axis=0)
    earlier = lax.broadcasted_iota(jnp.int32, (rows, rows), 0)
    later = lax.broadcasted_iota(jnp.int32, (rows, rows), 1)
    rank = jnp.dot(
        stacked.astype(BF), (earlier < later).astype(F32).astype(BF), preferred_element_type=F32
    )
    slot = lax.broadcasted_iota(jnp.int32, (slots, rows), 0).astype(F32)
    for k in range(len(metas)):
        for y in range(YS):
            i = k * YS + y
            here = (rank[i : i + 1, :] == slot) & (named[i] > 0.5)
            at = slice(y * slots, (y + 1) * slots)
            scaled = jnp.where(here, gates[i], 0.0)
            high = scaled.astype(BF)
            pick_ref[k, at, :] = here.astype(F32).astype(BF)
            high_ref[k, at, :] = high
            low_ref[k, at, :] = (scaled - high.astype(F32)).astype(BF)


def plan(group, slots, *metas):
    out = jax.ShapeDtypeStruct((len(metas), YS * slots, metas[0].shape[1]), BF)
    return pl.pallas_call(
        plan_kernel,
        out_shape=(out, out, out),
        in_specs=[pl.BlockSpec(memory_space=pltpu.SMEM)] + [pl.BlockSpec()] * len(metas),
        compiler_params=PARAMS,
        name="plan",
    )(group, *metas)


def gather_kernel(pieces, pick_ref, *refs):
    blocks, out_ref = refs[:-1], refs[-1]
    slots = out_ref.shape[2]
    for i in range(pick_ref.shape[0]):
        rows = jnp.concatenate([ref[...] for ref in blocks[i * pieces : (i + 1) * pieces]], axis=0)
        got = jnp.dot(pick_ref[i], rows, preferred_element_type=F32).astype(BF)
        for y in range(YS):
            out_ref[y, i] = got[y * slots : (y + 1) * slots]


def gather(pick, *blocks):
    sources, routes, _ = pick.shape
    width = blocks[0].shape[1]
    shape = (YS, sources, routes // YS)
    return pl.pallas_call(
        functools.partial(gather_kernel, len(blocks) // sources),
        grid=(width // TILE,),
        out_shape=jax.ShapeDtypeStruct(shape + (width,), BF),
        in_specs=[pl.BlockSpec(pick.shape, lambda j: (0, 0, 0))]
        + [pl.BlockSpec((b.shape[0], TILE), lambda j: (0, j)) for b in blocks],
        out_specs=pl.BlockSpec(shape + (TILE,), lambda j: (0, 0, 0, j)),
        compiler_params=PARAMS,
        name="gather",
    )(pick, *blocks)


def expert_kernel(place_ref, x_ref, *refs):
    ins, downs, outs = refs[0:4], refs[4:8], refs[8:-2]
    sums_ref, hidden_ref = refs[-2:]
    step = pl.program_id(0)
    parts = sums_ref.shape[0]
    half = parts // 2
    each = XS // len(outs)

    def columns(x, r):
        return pl.ds(pl.multiple_of((x * 4 + place_ref[r]) * BLOCK, BLOCK), BLOCK)

    @pl.when(step == 0)
    def _():
        sums_ref[...] = jnp.zeros_like(sums_ref)

    @pl.when(step < XS)
    def _():
        rows = [x_ref[:, columns(step, r)] for r in range(4)]
        for n in range(parts):
            sums_ref[n] += sum(
                jnp.dot(rows[r], ins[r][n], preferred_element_type=F32) for r in range(4)
            )

    @pl.when(step == XS)
    def _():
        for n in range(half):
            g, u = sums_ref[n], sums_ref[half + n]
            hidden_ref[n] = (g / (1.0 + jnp.exp(-g)) * u).astype(BF)

    for x in range(XS):

        @pl.when(step == XS + x)
        def _(x=x):
            for r in range(4):
                made = sum(
                    jnp.dot(hidden_ref[n], downs[r][n], preferred_element_type=F32)
                    for n in range(half)
                )
                outs[x // each][:, columns(x % each, r)] = made.astype(BF)


def expert(place, rows, packs, pieces):
    count, width = rows.shape
    half = packs[0].shape[1] // 3
    out = jax.ShapeDtypeStruct((count, width // pieces), BF)
    return pl.pallas_call(
        expert_kernel,
        grid_spec=pltpu.PrefetchScalarGridSpec(
            num_scalar_prefetch=1,
            grid=(2 * XS,),
            in_specs=[pl.BlockSpec((count, width), lambda s, p: (0, 0))]
            + [
                pl.BlockSpec(
                    (pl.Squeezed(), 2 * half, BLOCK, BLOCK),
                    lambda s, p: (jnp.minimum(s, XS - 1), 0, 0, 0),
                )
            ]
            * 4
            + [
                pl.BlockSpec(
                    (pl.Squeezed(), half, BLOCK, BLOCK),
                    lambda s, p: (jnp.maximum(s - XS, 0), 2, 0, 0),
                )
            ]
            * 4,
            out_specs=[pl.BlockSpec(out.shape, lambda s, p: (0, 0))] * pieces,
            scratch_shapes=[
                pltpu.VMEM((2 * half, count, BLOCK), F32),
                pltpu.VMEM((half, count, BLOCK), BF),
            ],
        ),
        out_shape=[out] * pieces,
        compiler_params=PARAMS,
        name="expert",
    )(place, rows, *packs, *packs)


def weighted(high_ref, low_ref, i, rows_ref):
    rows = jnp.concatenate([rows_ref[y, i] for y in range(YS)], axis=0)
    return sum(
        lax.dot_general(s[i], rows, (((0,), (0,)), ((), ())), preferred_element_type=F32)
        for s in (high_ref, low_ref)
    )


def split_kernel(high_ref, low_ref, rows_ref, top_ref, bottom_ref):
    total = weighted(high_ref, low_ref, 0, rows_ref).astype(BF)
    half = top_ref.shape[0]
    top_ref[...], bottom_ref[...] = total[:half], total[half:]


def add_kernel(high_ref, low_ref, rows_ref, top_ref, bottom_ref, below_ref, above_ref):
    half = top_ref.shape[0]
    below = weighted(high_ref, low_ref, 0, rows_ref)
    above = weighted(high_ref, low_ref, 1, rows_ref)
    below_ref[:half, :] = (below[:half] + top_ref[...].astype(F32)).astype(BF)
    below_ref[half:, :] = below[half:].astype(BF)
    above_ref[:half, :] = above[:half].astype(BF)
    above_ref[half:, :] = (above[half:] + bottom_ref[...].astype(F32)).astype(BF)


def last_kernel(high_ref, low_ref, rows_ref, *refs):
    left, right, out_ref = refs[0:2], refs[2:4], refs[4]
    total = weighted(high_ref, low_ref, 0, rows_ref)
    first = pl.program_id(0) < pl.num_programs(0) // 2

    @pl.when(first)
    def _():
        out_ref[...] = (total + left[0][...].astype(F32) + left[1][...].astype(F32)).astype(BF)

    @pl.when(jnp.logical_not(first))
    def _():
        out_ref[...] = (total + right[0][...].astype(F32) + right[1][...].astype(F32)).astype(BF)


def combine(kernel, plans, rows, more, counts):
    _, high, low = plans
    width = rows.shape[-1]
    table = pl.BlockSpec(high.shape, lambda j: (0, 0, 0))
    return pl.pallas_call(
        kernel,
        grid=(width // TILE,),
        out_shape=[jax.ShapeDtypeStruct((n, width), BF) for n in counts],
        in_specs=[table, table, pl.BlockSpec(rows.shape[:-1] + (TILE,), lambda j: (0, 0, 0, j))]
        + [pl.BlockSpec((a.shape[0], TILE), lambda j, at=at: (0, at(j))) for a, at in more],
        out_specs=[pl.BlockSpec((n, TILE), lambda j: (0, j)) for n in counts],
        compiler_params=PARAMS,
        name="combine",
    )(high, low, rows, *[a for a, _ in more])


def over_y(rows, shape):
    return lax.all_to_all(
        rows.reshape(YS, -1, rows.shape[-1]), "y", split_axis=0, concat_axis=0, tiled=True
    ).reshape(shape)


def on_device(tokens, route_ids, gate_values, w_gate_up, w_down):
    tok_rows, top = route_ids.shape
    model = tokens.shape[1]
    slots = 3 * tok_rows * top // (2 * ZH * YS)
    half = tok_rows // 2
    swap = [(0, 1), (1, 0)]
    group = lax.axis_index("zh").reshape(1)
    barrier = lax.optimization_barrier
    pack = pack_shards(w_gate_up[0], w_down[0])
    meta = jnp.concatenate([route_ids.astype(F32).T, gate_values.T], axis=0)

    near = [lax.ppermute(tokens, "zh", ring(k)) for k in (1, 3)]
    near_metas = [lax.ppermute(meta, "zh", ring(k)) for k in (1, 3)]
    swapped = lax.ppermute(pack, "zl", swap)
    mine = lax.all_gather(pack, "x")
    own = plan(group, slots, meta)
    arrived_own = over_y(gather(own[0], tokens), (-1, model))
    near, near_metas, swapped, arrived_own = barrier((near, near_metas, swapped, arrived_own))
    other = lax.all_gather(swapped, "x")

    sides = plan(group, slots, *near_metas)
    top, bottom, sent = barrier((near[0][:half], near[1][half:], gather(sides[0], *near)))
    arrived_sides = over_y(sent, (-1, model))
    far = [lax.ppermute(top, "zh", ring(1)), lax.ppermute(bottom, "zh", ring(3))]
    far_meta = lax.ppermute(near_metas[0], "zh", ring(1))
    far, far_meta, mine, arrived_sides = barrier((far, far_meta, mine, arrived_sides))
    mine_swapped = lax.ppermute(mine, "core", swap)
    across = plan(group, slots, far_meta)
    arrived_across = over_y(gather(across[0], *far), (-1, model))
    packs = [mine, mine_swapped, other, lax.ppermute(other, "core", swap)]
    zl, core = lax.axis_index("zl"), lax.axis_index("core")
    place = jnp.stack([zl * 2 + core, zl * 2 + 1 - core, (1 - zl) * 2 + core, (1 - zl) * 2 + 1 - core])

    made_sides = expert(place, arrived_sides, packs, 2)
    (made_own,) = expert(place, arrived_own, packs, 1)
    made_sides, made_own, arrived_across = barrier((made_sides, made_own, arrived_across))
    (made,) = expert(place, arrived_across, packs, 1)

    back = over_y(made, (YS, 1, slots, model))
    parts = combine(split_kernel, across, back, [], (half, half))
    passed = [lax.ppermute(parts[0], "zh", ring(3)), lax.ppermute(parts[1], "zh", ring(1))]
    home = []
    for piece in range(2):
        if piece == 0:
            rows, back = barrier((made_sides[0], back))
        else:
            rows, passed = barrier((made_sides[1], passed))
        back = over_y(rows, (YS, 2, slots, model // 2))
        shift = lambda j, at=piece * (model // 2 // TILE): j + at
        below, above = combine(
            add_kernel, sides, back, [(p, shift) for p in passed], (tok_rows, tok_rows)
        )
        if piece == 1:
            made_own, home, below = barrier((made_own, home, below))
        home = home + [lax.ppermute(below, "zh", ring(3)), lax.ppermute(above, "zh", ring(1))]
    back = over_y(made_own, (YS, 1, slots, model))
    steps = model // 2 // TILE
    left, right = lambda j: jnp.minimum(j, steps - 1), lambda j: jnp.maximum(j - steps, 0)
    more = [(home[0], left), (home[1], left), (home[2], right), (home[3], right)]
    return combine(last_kernel, own, back, more, (tok_rows,))[0]


def solution(mesh):
    split = Mesh(mesh.devices.reshape(ZH, YS, XS, 2, 2), ("zh", "y", "x", "zl", "core"))
    owner, shard = ("zh", "y"), ("x", "zl", "core")
    every = owner + shard
    in_specs = (P(every, None),) * 3 + (P(owner, shard, None), P(owner, None, shard))
    return jax.shard_map(
        on_device, mesh=split, in_specs=in_specs, out_specs=P(every, None), check_vma=False
    )
```

```python
import functools

import jax
import jax.numpy as jnp
from jax import lax
from jax.experimental import pallas as pl
from jax.experimental.pallas import tpu as pltpu
from jax.sharding import Mesh, PartitionSpec as P

BF, F32 = jnp.bfloat16, jnp.float32
ZH, YS, XS = 4, 4, 4
PARAMS = pltpu.CompilerParams(vmem_limit_bytes=56 << 20)
BLOCK = 256
TILE = 2048


def ring(step):
    return [(i, (i + step) % ZH) for i in range(ZH)]


def pack_kernel(up_ref, down_ref, out_ref):
    step = pl.program_id(0)

    @pl.when(step < 2)
    def _():
        for n in range(3):
            out_ref[n] = up_ref[:, n * BLOCK : (n + 1) * BLOCK]

    @pl.when(step == 2)
    def _():
        for n in range(3):
            out_ref[n] = down_ref[n * BLOCK : (n + 1) * BLOCK, :]


def pack_shards(up, down):
    return pl.pallas_call(
        pack_kernel,
        grid=(3,),
        out_shape=jax.ShapeDtypeStruct((9, BLOCK, BLOCK), BF),
        in_specs=[
            pl.BlockSpec((BLOCK, 3 * BLOCK), lambda s: (0, jnp.minimum(s, 1))),
            pl.BlockSpec((3 * BLOCK, BLOCK), lambda s: (0, 0)),
        ],
        out_specs=pl.BlockSpec((3, BLOCK, BLOCK), lambda s: (s, 0, 0)),
        compiler_params=PARAMS,
        name="pack",
    )(up, down)


def plan_kernel(group_ref, *refs):
    metas, (pick_ref, high_ref, low_ref) = refs[:-3], refs[-3:]
    rows = metas[0].shape[1]
    slots = pick_ref.shape[1] // YS
    group = group_ref[0]
    named, gates = [], []
    for meta_ref in metas:
        ids, weights = meta_ref[0:4, :], meta_ref[4:8, :]
        for y in range(YS):
            match = ids == (group * YS + y).astype(F32)
            named.append(jnp.sum(match.astype(F32), axis=0, keepdims=True))
            gates.append(jnp.sum(jnp.where(match, weights, 0.0), axis=0, keepdims=True))
    stacked = jnp.concatenate(named, axis=0)
    earlier = lax.broadcasted_iota(jnp.int32, (rows, rows), 0)
    later = lax.broadcasted_iota(jnp.int32, (rows, rows), 1)
    rank = jnp.dot(
        stacked.astype(BF), (earlier < later).astype(F32).astype(BF), preferred_element_type=F32
    )
    slot = lax.broadcasted_iota(jnp.int32, (slots, rows), 0).astype(F32)
    for k in range(len(metas)):
        for y in range(YS):
            i = k * YS + y
            here = (rank[i : i + 1, :] == slot) & (named[i] > 0.5)
            at = slice(y * slots, (y + 1) * slots)
            scaled = jnp.where(here, gates[i], 0.0)
            high = scaled.astype(BF)
            pick_ref[k, at, :] = here.astype(F32).astype(BF)
            high_ref[k, at, :] = high
            low_ref[k, at, :] = (scaled - high.astype(F32)).astype(BF)


def plan(group, slots, *metas):
    out = jax.ShapeDtypeStruct((len(metas), YS * slots, metas[0].shape[1]), BF)
    return pl.pallas_call(
        plan_kernel,
        out_shape=(out, out, out),
        in_specs=[pl.BlockSpec(memory_space=pltpu.SMEM)] + [pl.BlockSpec()] * len(metas),
        compiler_params=PARAMS,
        name="plan",
    )(group, *metas)


def gather_kernel(pieces, pick_ref, *refs):
    blocks, out_ref = refs[:-1], refs[-1]
    slots = out_ref.shape[2]
    for i in range(pick_ref.shape[0]):
        rows = jnp.concatenate([ref[...] for ref in blocks[i * pieces : (i + 1) * pieces]], axis=0)
        got = jnp.dot(pick_ref[i], rows, preferred_element_type=F32).astype(BF)
        for y in range(YS):
            out_ref[y, i] = got[y * slots : (y + 1) * slots]


def gather(pick, *blocks):
    sources, routes, _ = pick.shape
    width = blocks[0].shape[1]
    shape = (YS, sources, routes // YS)
    return pl.pallas_call(
        functools.partial(gather_kernel, len(blocks) // sources),
        grid=(width // TILE,),
        out_shape=jax.ShapeDtypeStruct(shape + (width,), BF),
        in_specs=[pl.BlockSpec(pick.shape, lambda j: (0, 0, 0))]
        + [pl.BlockSpec((b.shape[0], TILE), lambda j: (0, j)) for b in blocks],
        out_specs=pl.BlockSpec(shape + (TILE,), lambda j: (0, 0, 0, j)),
        compiler_params=PARAMS,
        name="gather",
    )(pick, *blocks)


def expert_kernel(place_ref, x_ref, *refs):
    ins, downs, outs = refs[0:4], refs[4:8], refs[8:-2]
    sums_ref, hidden_ref = refs[-2:]
    step = pl.program_id(0)
    parts = sums_ref.shape[0]
    half = parts // 2
    each = XS // len(outs)

    def columns(x, r):
        return pl.ds(pl.multiple_of((x * 4 + place_ref[r]) * BLOCK, BLOCK), BLOCK)

    @pl.when(step == 0)
    def _():
        sums_ref[...] = jnp.zeros_like(sums_ref)

    @pl.when(step < XS)
    def _():
        rows = [x_ref[:, columns(step, r)] for r in range(4)]
        for n in range(parts):
            sums_ref[n] += sum(
                jnp.dot(rows[r], ins[r][n], preferred_element_type=F32) for r in range(4)
            )

    @pl.when(step == XS)
    def _():
        for n in range(half):
            g, u = sums_ref[n], sums_ref[half + n]
            hidden_ref[n] = (g / (1.0 + jnp.exp(-g)) * u).astype(BF)

    for x in range(XS):

        @pl.when(step == XS + x)
        def _(x=x):
            for r in range(4):
                made = sum(
                    jnp.dot(hidden_ref[n], downs[r][n], preferred_element_type=F32)
                    for n in range(half)
                )
                outs[x // each][:, columns(x % each, r)] = made.astype(BF)


def expert(place, rows, packs, pieces):
    count, width = rows.shape
    half = packs[0].shape[1] // 3
    out = jax.ShapeDtypeStruct((count, width // pieces), BF)
    return pl.pallas_call(
        expert_kernel,
        grid_spec=pltpu.PrefetchScalarGridSpec(
            num_scalar_prefetch=1,
            grid=(2 * XS,),
            in_specs=[pl.BlockSpec((count, width), lambda s, p: (0, 0))]
            + [
                pl.BlockSpec(
                    (pl.Squeezed(), 2 * half, BLOCK, BLOCK),
                    lambda s, p: (jnp.minimum(s, XS - 1), 0, 0, 0),
                )
            ]
            * 4
            + [
                pl.BlockSpec(
                    (pl.Squeezed(), half, BLOCK, BLOCK),
                    lambda s, p: (jnp.maximum(s - XS, 0), 2, 0, 0),
                )
            ]
            * 4,
            out_specs=[pl.BlockSpec(out.shape, lambda s, p: (0, 0))] * pieces,
            scratch_shapes=[
                pltpu.VMEM((2 * half, count, BLOCK), F32),
                pltpu.VMEM((half, count, BLOCK), BF),
            ],
        ),
        out_shape=[out] * pieces,
        compiler_params=PARAMS,
        name="expert",
    )(place, rows, *packs, *packs)


def weighted(high_ref, low_ref, i, rows_ref):
    rows = jnp.concatenate([rows_ref[y, i] for y in range(YS)], axis=0)
    return sum(
        lax.dot_general(s[i], rows, (((0,), (0,)), ((), ())), preferred_element_type=F32)
        for s in (high_ref, low_ref)
    )


def split_kernel(high_ref, low_ref, rows_ref, top_ref, bottom_ref):
    total = weighted(high_ref, low_ref, 0, rows_ref).astype(BF)
    half = top_ref.shape[0]
    top_ref[...], bottom_ref[...] = total[:half], total[half:]


def add_kernel(high_ref, low_ref, rows_ref, top_ref, bottom_ref, below_ref, above_ref):
    half = top_ref.shape[0]
    below = weighted(high_ref, low_ref, 0, rows_ref)
    above = weighted(high_ref, low_ref, 1, rows_ref)
    below_ref[:half, :] = (below[:half] + top_ref[...].astype(F32)).astype(BF)
    below_ref[half:, :] = below[half:].astype(BF)
    above_ref[:half, :] = above[:half].astype(BF)
    above_ref[half:, :] = (above[half:] + bottom_ref[...].astype(F32)).astype(BF)


def last_kernel(high_ref, low_ref, rows_ref, *refs):
    left, right, out_ref = refs[0:2], refs[2:4], refs[4]
    total = weighted(high_ref, low_ref, 0, rows_ref)
    first = pl.program_id(0) < pl.num_programs(0) // 2

    @pl.when(first)
    def _():
        out_ref[...] = (total + left[0][...].astype(F32) + left[1][...].astype(F32)).astype(BF)

    @pl.when(jnp.logical_not(first))
    def _():
        out_ref[...] = (total + right[0][...].astype(F32) + right[1][...].astype(F32)).astype(BF)


def combine(kernel, plans, rows, first, steps, more, counts):
    _, high, low = plans
    table = pl.BlockSpec(high.shape, lambda j: (0, 0, 0))
    return pl.pallas_call(
        kernel,
        grid=(steps,),
        out_shape=[jax.ShapeDtypeStruct((n, steps * TILE), BF) for n in counts],
        in_specs=[
            table,
            table,
            pl.BlockSpec(rows.shape[:-1] + (TILE,), lambda j: (0, 0, 0, first + j)),
        ]
        + [pl.BlockSpec(a.shape, lambda j: (0, 0)) for a in more],
        out_specs=[pl.BlockSpec((n, TILE), lambda j: (0, j)) for n in counts],
        compiler_params=PARAMS,
        name="combine",
    )(high, low, rows, *more)


def over_y(rows, shape):
    return lax.all_to_all(
        rows.reshape(YS, -1, rows.shape[-1]), "y", split_axis=0, concat_axis=0, tiled=True
    ).reshape(shape)


def on_device(tokens, route_ids, gate_values, w_gate_up, w_down):
    tok_rows, top = route_ids.shape
    model = tokens.shape[1]
    slots = 3 * tok_rows * top // (2 * ZH * YS)
    half = tok_rows // 2
    swap = [(0, 1), (1, 0)]
    group = lax.axis_index("zh").reshape(1)
    barrier = lax.optimization_barrier
    pack = pack_shards(w_gate_up[0], w_down[0])
    meta = jnp.concatenate([route_ids.astype(F32).T, gate_values.T], axis=0)

    near = [lax.ppermute(tokens, "zh", ring(k)) for k in (1, 3)]
    near_metas = [lax.ppermute(meta, "zh", ring(k)) for k in (1, 3)]
    swapped = lax.ppermute(pack, "zl", swap)
    mine = lax.all_gather(pack, "x")
    own = plan(group, slots, meta)
    arrived_own = over_y(gather(own[0], tokens), (-1, model))
    near, near_metas, swapped, arrived_own = barrier((near, near_metas, swapped, arrived_own))
    other = lax.all_gather(swapped, "x")

    sides = plan(group, slots, *near_metas)
    arrived_sides = over_y(gather(sides[0], *near), (-1, model))
    far = [lax.ppermute(near[0][:half], "zh", ring(1)), lax.ppermute(near[1][half:], "zh", ring(3))]
    far_meta = lax.ppermute(near_metas[0], "zh", ring(1))
    across = plan(group, slots, far_meta)
    sent, mine, arrived_sides = barrier((gather(across[0], *far), mine, arrived_sides))
    mine_swapped = lax.ppermute(mine, "core", swap)
    arrived_across = over_y(sent, (-1, model))
    packs = [mine, mine_swapped, other, lax.ppermute(other, "core", swap)]
    zl, core = lax.axis_index("zl"), lax.axis_index("core")
    place = jnp.stack([zl * 2 + core, zl * 2 + 1 - core, (1 - zl) * 2 + core, (1 - zl) * 2 + 1 - core])

    made_sides = expert(place, arrived_sides, packs, 2)
    made_sides, arrived_across = barrier((made_sides, arrived_across))
    (made,) = expert(place, arrived_across, packs, 1)

    back = over_y(made, (YS, 1, slots, model))
    pieces = range(model // TILE)
    parts = [combine(split_kernel, across, back, p, 1, [], (half, half)) for p in pieces]
    passed = [
        [lax.ppermute(top, "zh", ring(3)), lax.ppermute(bottom, "zh", ring(1))] for top, bottom in parts
    ]
    arrived_own, parts = barrier((arrived_own, parts))
    (made_own,) = expert(place, arrived_own, packs, 1)
    home, rows = [], made_sides[0]
    for p in pieces:
        rows, back = barrier((rows, back))
        back = over_y(rows, (YS, 2, slots, TILE))
        if p == 0:
            rows, passed[0], made_own = barrier((made_sides[1], passed[0], made_own))
            back, passed[1] = barrier((back, passed[1]))
        below, above = combine(add_kernel, sides, back, 0, 1, passed[p], (tok_rows, tok_rows))
        if p == 1:
            made_own, home, below, above = barrier((made_own, home, below, above))
        home = home + [lax.ppermute(below, "zh", ring(3)), lax.ppermute(above, "zh", ring(1))]
    back = over_y(made_own, (YS, 1, slots, model))
    return combine(last_kernel, own, back, 0, len(pieces), home, (tok_rows,))[0]


def solution(mesh):
    split = Mesh(mesh.devices.reshape(ZH, YS, XS, 2, 2), ("zh", "y", "x", "zl", "core"))
    owner, shard = ("zh", "y"), ("x", "zl", "core")
    every = owner + shard
    in_specs = (P(every, None),) * 3 + (P(owner, shard, None), P(owner, None, shard))
    return jax.shard_map(
        on_device, mesh=split, in_specs=in_specs, out_specs=P(every, None), check_vma=False
    )
```

```python
import functools

import jax
import jax.numpy as jnp
from jax import lax
from jax.experimental import pallas as pl
from jax.experimental.pallas import tpu as pltpu
from jax.sharding import Mesh, PartitionSpec as P

BF, F32 = jnp.bfloat16, jnp.float32
ZH, YS, XS = 4, 4, 4
PARAMS = pltpu.CompilerParams(vmem_limit_bytes=56 << 20)
BLOCK = 256
TILE = 2048


def ring(step):
    return [(i, (i + step) % ZH) for i in range(ZH)]


def pack_kernel(up_ref, down_ref, out_ref):
    step = pl.program_id(0)

    @pl.when(step < 2)
    def _():
        for n in range(3):
            out_ref[n] = up_ref[:, n * BLOCK : (n + 1) * BLOCK]

    @pl.when(step == 2)
    def _():
        for n in range(3):
            out_ref[n] = down_ref[n * BLOCK : (n + 1) * BLOCK, :]


def pack_shards(up, down):
    return pl.pallas_call(
        pack_kernel,
        grid=(3,),
        out_shape=jax.ShapeDtypeStruct((9, BLOCK, BLOCK), BF),
        in_specs=[
            pl.BlockSpec((BLOCK, 3 * BLOCK), lambda s: (0, jnp.minimum(s, 1))),
            pl.BlockSpec((3 * BLOCK, BLOCK), lambda s: (0, 0)),
        ],
        out_specs=pl.BlockSpec((3, BLOCK, BLOCK), lambda s: (s, 0, 0)),
        compiler_params=PARAMS,
        name="pack",
    )(up, down)


def plan_kernel(group_ref, *refs):
    metas, (pick_ref, high_ref, low_ref) = refs[:-3], refs[-3:]
    rows = metas[0].shape[1]
    slots = pick_ref.shape[1] // YS
    group = group_ref[0]
    named, gates = [], []
    for meta_ref in metas:
        ids, weights = meta_ref[0:4, :], meta_ref[4:8, :]
        for y in range(YS):
            match = ids == (group * YS + y).astype(F32)
            named.append(jnp.sum(match.astype(F32), axis=0, keepdims=True))
            gates.append(jnp.sum(jnp.where(match, weights, 0.0), axis=0, keepdims=True))
    stacked = jnp.concatenate(named, axis=0)
    earlier = lax.broadcasted_iota(jnp.int32, (rows, rows), 0)
    later = lax.broadcasted_iota(jnp.int32, (rows, rows), 1)
    rank = jnp.dot(
        stacked.astype(BF), (earlier < later).astype(F32).astype(BF), preferred_element_type=F32
    )
    slot = lax.broadcasted_iota(jnp.int32, (slots, rows), 0).astype(F32)
    for k in range(len(metas)):
        for y in range(YS):
            i = k * YS + y
            here = (rank[i : i + 1, :] == slot) & (named[i] > 0.5)
            at = slice(y * slots, (y + 1) * slots)
            scaled = jnp.where(here, gates[i], 0.0)
            high = scaled.astype(BF)
            pick_ref[k, at, :] = here.astype(F32).astype(BF)
            high_ref[k, at, :] = high
            low_ref[k, at, :] = (scaled - high.astype(F32)).astype(BF)


def plan(group, slots, *metas):
    out = jax.ShapeDtypeStruct((len(metas), YS * slots, metas[0].shape[1]), BF)
    return pl.pallas_call(
        plan_kernel,
        out_shape=(out, out, out),
        in_specs=[pl.BlockSpec(memory_space=pltpu.SMEM)] + [pl.BlockSpec()] * len(metas),
        compiler_params=PARAMS,
        name="plan",
    )(group, *metas)


def gather_kernel(counts, pick_ref, *refs):
    blocks, out_ref = refs[:-1], refs[-1]
    sources = pick_ref.shape[0]
    slots = out_ref.shape[2]
    halves, per_source = counts
    width = out_ref.shape[3] // halves
    for h in range(halves):
        for i in range(sources):
            first = (h * sources + i) * per_source
            rows = jnp.concatenate([ref[...] for ref in blocks[first : first + per_source]], axis=0)
            got = jnp.dot(pick_ref[i], rows, preferred_element_type=F32).astype(BF)
            for y in range(YS):
                out_ref[y, i, :, h * width : (h + 1) * width] = got[y * slots : (y + 1) * slots]


def gather(pick, blocks):
    sources, routes, _ = pick.shape
    counts = len(blocks), len(blocks[0][0])
    flat = [piece for part in blocks for source in part for piece in source]
    width = sum(part[0][0].shape[1] for part in blocks)
    return pl.pallas_call(
        functools.partial(gather_kernel, counts),
        out_shape=jax.ShapeDtypeStruct((YS, sources, routes // YS, width), BF),
        compiler_params=PARAMS,
        name="gather",
    )(pick, *flat)


def expert_kernel(given, place_ref, *refs):
    rows, refs = refs[:given], refs[given:]
    ins, downs, outs = refs[0:4], refs[4:8], refs[8:-2]
    sums_ref, hidden_ref = refs[-2:]
    step = pl.program_id(0)
    parts = sums_ref.shape[0]
    half = parts // 2
    taken, each = XS // given, XS // len(outs)

    def columns(x, r):
        return pl.ds(pl.multiple_of((x * 4 + place_ref[r]) * BLOCK, BLOCK), BLOCK)

    @pl.when(step == 0)
    def _():
        sums_ref[...] = jnp.zeros_like(sums_ref)

    for piece in range(given):

        @pl.when((step >= piece * taken) & (step < (piece + 1) * taken))
        def _(piece=piece):
            x = [rows[piece][:, columns(step - piece * taken, r)] for r in range(4)]
            for n in range(parts):
                sums_ref[n] += sum(
                    jnp.dot(x[r], ins[r][n], preferred_element_type=F32) for r in range(4)
                )

    @pl.when(step == XS)
    def _():
        for n in range(half):
            g, u = sums_ref[n], sums_ref[half + n]
            hidden_ref[n] = (g / (1.0 + jnp.exp(-g)) * u).astype(BF)

    for x in range(XS):

        @pl.when(step == XS + x)
        def _(x=x):
            for r in range(4):
                made = sum(
                    jnp.dot(hidden_ref[n], downs[r][n], preferred_element_type=F32)
                    for n in range(half)
                )
                outs[x // each][:, columns(x % each, r)] = made.astype(BF)


def expert(place, rows, packs, pieces):
    count = rows[0].shape[0]
    width = sum(r.shape[1] for r in rows)
    half = packs[0].shape[1] // 3
    out = jax.ShapeDtypeStruct((count, width // pieces), BF)
    return pl.pallas_call(
        functools.partial(expert_kernel, len(rows)),
        grid_spec=pltpu.PrefetchScalarGridSpec(
            num_scalar_prefetch=1,
            grid=(2 * XS,),
            in_specs=[pl.BlockSpec(r.shape, lambda s, p: (0, 0)) for r in rows]
            + [
                pl.BlockSpec(
                    (pl.Squeezed(), 2 * half, BLOCK, BLOCK),
                    lambda s, p: (jnp.minimum(s, XS - 1), 0, 0, 0),
                )
            ]
            * 4
            + [
                pl.BlockSpec(
                    (pl.Squeezed(), half, BLOCK, BLOCK),
                    lambda s, p: (jnp.maximum(s - XS, 0), 2, 0, 0),
                )
            ]
            * 4,
            out_specs=[pl.BlockSpec(out.shape, lambda s, p: (0, 0))] * pieces,
            scratch_shapes=[
                pltpu.VMEM((2 * half, count, BLOCK), F32),
                pltpu.VMEM((half, count, BLOCK), BF),
            ],
        ),
        out_shape=[out] * pieces,
        compiler_params=PARAMS,
        name="expert",
    )(place, *rows, *packs, *packs)


def weighted(high_ref, low_ref, i, rows_ref):
    rows = jnp.concatenate([rows_ref[y, i] for y in range(YS)], axis=0)
    return sum(
        lax.dot_general(s[i], rows, (((0,), (0,)), ((), ())), preferred_element_type=F32)
        for s in (high_ref, low_ref)
    )


def split_kernel(high_ref, low_ref, rows_ref, top_ref, bottom_ref):
    total = weighted(high_ref, low_ref, 0, rows_ref).astype(BF)
    half = top_ref.shape[0]
    top_ref[...], bottom_ref[...] = total[:half], total[half:]


def add_kernel(high_ref, low_ref, rows_ref, top_ref, bottom_ref, below_ref, above_ref):
    half = top_ref.shape[0]
    below = weighted(high_ref, low_ref, 0, rows_ref)
    above = weighted(high_ref, low_ref, 1, rows_ref)
    below_ref[:half, :] = (below[:half] + top_ref[...].astype(F32)).astype(BF)
    below_ref[half:, :] = below[half:].astype(BF)
    above_ref[:half, :] = above[:half].astype(BF)
    above_ref[half:, :] = (above[half:] + bottom_ref[...].astype(F32)).astype(BF)


def last_kernel(high_ref, low_ref, rows_ref, *refs):
    left, right, out_ref = refs[0:2], refs[2:4], refs[4]
    total = weighted(high_ref, low_ref, 0, rows_ref)
    first = pl.program_id(0) < pl.num_programs(0) // 2

    @pl.when(first)
    def _():
        out_ref[...] = (total + left[0][...].astype(F32) + left[1][...].astype(F32)).astype(BF)

    @pl.when(jnp.logical_not(first))
    def _():
        out_ref[...] = (total + right[0][...].astype(F32) + right[1][...].astype(F32)).astype(BF)


def combine(kernel, plans, rows, first, steps, more, counts):
    _, high, low = plans
    table = pl.BlockSpec(high.shape, lambda j: (0, 0, 0))
    return pl.pallas_call(
        kernel,
        grid=(steps,),
        out_shape=[jax.ShapeDtypeStruct((n, steps * TILE), BF) for n in counts],
        in_specs=[
            table,
            table,
            pl.BlockSpec(rows.shape[:-1] + (TILE,), lambda j: (0, 0, 0, first + j)),
        ]
        + [pl.BlockSpec(a.shape, lambda j: (0, 0)) for a in more],
        out_specs=[pl.BlockSpec((n, TILE), lambda j: (0, j)) for n in counts],
        compiler_params=PARAMS,
        name="combine",
    )(high, low, rows, *more)


def over_y(rows, shape):
    return lax.all_to_all(
        rows.reshape(YS, -1, rows.shape[-1]), "y", split_axis=0, concat_axis=0, tiled=True
    ).reshape(shape)


def on_device(tokens, route_ids, gate_values, w_gate_up, w_down):
    tok_rows, top = route_ids.shape
    model = tokens.shape[1]
    slots = 3 * tok_rows * top // (2 * ZH * YS)
    half = tok_rows // 2
    swap = [(0, 1), (1, 0)]
    group = lax.axis_index("zh").reshape(1)
    barrier = lax.optimization_barrier
    pack = pack_shards(w_gate_up[0], w_down[0])
    meta = jnp.concatenate([route_ids.astype(F32).T, gate_values.T], axis=0)

    pieces = range(model // TILE)
    token_parts = [tokens[:, p * TILE : (p + 1) * TILE] for p in pieces]
    near_metas = [lax.ppermute(meta, "zh", ring(k)) for k in (1, 3)]
    near = [[lax.ppermute(t, "zh", ring(k)) for k in (1, 3)] for t in token_parts]
    swapped = lax.ppermute(pack, "zl", swap)
    mine = lax.all_gather(pack, "x")
    own = plan(group, slots, meta)
    arrived_own = over_y(gather(own[0], [[[tokens]]]), (-1, model))
    sides = plan(group, slots, *near_metas)
    near[0], sides, swapped, arrived_own = barrier((near[0], sides, swapped, arrived_own))
    other = lax.all_gather(swapped, "x")
    far_meta = lax.ppermute(near_metas[0], "zh", ring(1))

    arrived_sides, far = [], []
    for p in pieces:
        arrived_sides.append(over_y(gather(sides[0], [[[t] for t in near[p]]]), (-1, TILE)))
        below, above = near[p]
        far.append(
            [lax.ppermute(below[:half], "zh", ring(1)), lax.ppermute(above[half:], "zh", ring(3))]
        )
        if p == 0:
            near[1], arrived_sides, far = barrier((near[1], arrived_sides, far))
    across = plan(group, slots, far_meta)
    sent, mine, arrived_sides = barrier((gather(across[0], [[f] for f in far]), mine, arrived_sides))
    mine_swapped = lax.ppermute(mine, "core", swap)
    arrived_across = over_y(sent, (-1, model))
    packs = [mine, mine_swapped, other, lax.ppermute(other, "core", swap)]
    zl, core = lax.axis_index("zl"), lax.axis_index("core")
    place = jnp.stack([zl * 2 + core, zl * 2 + 1 - core, (1 - zl) * 2 + core, (1 - zl) * 2 + 1 - core])

    made_sides = expert(place, arrived_sides, packs, 2)
    made_sides, arrived_across = barrier((made_sides, arrived_across))
    (made,) = expert(place, [arrived_across], packs, 1)
    made, arrived_own = barrier((made, arrived_own))
    (made_own,) = expert(place, [arrived_own], packs, 1)

    back, made_own = barrier((over_y(made, (YS, 1, slots, model)), made_own))
    parts = [combine(split_kernel, across, back, p, 1, [], (half, half)) for p in pieces]
    passed = [
        [lax.ppermute(top, "zh", ring(3)), lax.ppermute(bottom, "zh", ring(1))] for top, bottom in parts
    ]
    home, rows = [], made_sides[0]
    for p in pieces:
        rows, back = barrier((rows, back))
        back = over_y(rows, (YS, 2, slots, TILE))
        if p == 0:
            rows, passed[0] = barrier((made_sides[1], passed[0]))
            back, passed[1] = barrier((back, passed[1]))
        below, above = combine(add_kernel, sides, back, 0, 1, passed[p], (tok_rows, tok_rows))
        if p == 1:
            made_own, home, below, above = barrier((made_own, home, below, above))
        home = home + [lax.ppermute(below, "zh", ring(3)), lax.ppermute(above, "zh", ring(1))]
    back = over_y(made_own, (YS, 1, slots, model))
    return combine(last_kernel, own, back, 0, len(pieces), home, (tok_rows,))[0]


def solution(mesh):
    split = Mesh(mesh.devices.reshape(ZH, YS, XS, 2, 2), ("zh", "y", "x", "zl", "core"))
    owner, shard = ("zh", "y"), ("x", "zl", "core")
    every = owner + shard
    in_specs = (P(every, None),) * 3 + (P(owner, shard, None), P(owner, None, shard))
    return jax.shard_map(
        on_device, mesh=split, in_specs=in_specs, out_specs=P(every, None), check_vma=False
    )
```

```python
import functools

import jax
import jax.numpy as jnp
from jax import lax
from jax.experimental import pallas as pl
from jax.experimental.pallas import tpu as pltpu
from jax.sharding import Mesh, PartitionSpec as P

BF, F32 = jnp.bfloat16, jnp.float32
ZH, YS, XS = 4, 4, 4
PARAMS = pltpu.CompilerParams(vmem_limit_bytes=56 << 20)
BLOCK = 256
TILE = 2048


def ring(step):
    return [(i, (i + step) % ZH) for i in range(ZH)]


def pack_kernel(up_ref, down_ref, out_ref):
    step = pl.program_id(0)

    @pl.when(step < 2)
    def _():
        for n in range(3):
            out_ref[n] = up_ref[:, n * BLOCK : (n + 1) * BLOCK]

    @pl.when(step == 2)
    def _():
        for n in range(3):
            out_ref[n] = down_ref[n * BLOCK : (n + 1) * BLOCK, :]


def pack_shards(up, down):
    return pl.pallas_call(
        pack_kernel,
        grid=(3,),
        out_shape=jax.ShapeDtypeStruct((9, BLOCK, BLOCK), BF),
        in_specs=[
            pl.BlockSpec((BLOCK, 3 * BLOCK), lambda s: (0, jnp.minimum(s, 1))),
            pl.BlockSpec((3 * BLOCK, BLOCK), lambda s: (0, 0)),
        ],
        out_specs=pl.BlockSpec((3, BLOCK, BLOCK), lambda s: (s, 0, 0)),
        compiler_params=PARAMS,
        name="pack",
    )(up, down)


def plan_kernel(group_ref, *refs):
    metas, (pick_ref, high_ref, low_ref) = refs[:-3], refs[-3:]
    rows = metas[0].shape[1]
    slots = pick_ref.shape[1] // YS
    group = group_ref[0]
    named, gates = [], []
    for meta_ref in metas:
        ids, weights = meta_ref[0:4, :], meta_ref[4:8, :]
        for y in range(YS):
            match = ids == (group * YS + y).astype(F32)
            named.append(jnp.sum(match.astype(F32), axis=0, keepdims=True))
            gates.append(jnp.sum(jnp.where(match, weights, 0.0), axis=0, keepdims=True))
    stacked = jnp.concatenate(named, axis=0)
    earlier = lax.broadcasted_iota(jnp.int32, (rows, rows), 0)
    later = lax.broadcasted_iota(jnp.int32, (rows, rows), 1)
    rank = jnp.dot(
        stacked.astype(BF), (earlier < later).astype(F32).astype(BF), preferred_element_type=F32
    )
    slot = lax.broadcasted_iota(jnp.int32, (slots, rows), 0).astype(F32)
    for k in range(len(metas)):
        for y in range(YS):
            i = k * YS + y
            here = (rank[i : i + 1, :] == slot) & (named[i] > 0.5)
            at = slice(y * slots, (y + 1) * slots)
            scaled = jnp.where(here, gates[i], 0.0)
            high = scaled.astype(BF)
            pick_ref[k, at, :] = here.astype(F32).astype(BF)
            high_ref[k, at, :] = high
            low_ref[k, at, :] = (scaled - high.astype(F32)).astype(BF)


def plan(group, slots, *metas):
    out = jax.ShapeDtypeStruct((len(metas), YS * slots, metas[0].shape[1]), BF)
    return pl.pallas_call(
        plan_kernel,
        out_shape=(out, out, out),
        in_specs=[pl.BlockSpec(memory_space=pltpu.SMEM)] + [pl.BlockSpec()] * len(metas),
        compiler_params=PARAMS,
        name="plan",
    )(group, *metas)


def gather_kernel(counts, pick_ref, *refs):
    blocks, out_ref = refs[:-1], refs[-1]
    sources = pick_ref.shape[0]
    slots = out_ref.shape[2]
    halves, per_source = counts
    width = out_ref.shape[3] // halves
    for h in range(halves):
        for i in range(sources):
            first = (h * sources + i) * per_source
            rows = jnp.concatenate([ref[...] for ref in blocks[first : first + per_source]], axis=0)
            got = jnp.dot(pick_ref[i], rows, preferred_element_type=F32).astype(BF)
            for y in range(YS):
                out_ref[y, i, :, h * width : (h + 1) * width] = got[y * slots : (y + 1) * slots]


def gather(pick, blocks):
    sources, routes, _ = pick.shape
    counts = len(blocks), len(blocks[0][0])
    flat = [piece for part in blocks for source in part for piece in source]
    width = sum(part[0][0].shape[1] for part in blocks)
    return pl.pallas_call(
        functools.partial(gather_kernel, counts),
        out_shape=jax.ShapeDtypeStruct((YS, sources, routes // YS, width), BF),
        compiler_params=PARAMS,
        name="gather",
    )(pick, *flat)


def expert_kernel(given, place_ref, *refs):
    rows, refs = refs[:given], refs[given:]
    ins, downs, outs = refs[0:4], refs[4:8], refs[8:-2]
    sums_ref, hidden_ref = refs[-2:]
    step = pl.program_id(0)
    parts = sums_ref.shape[0]
    half = parts // 2
    taken, each = XS // given, XS // len(outs)

    def columns(x, r):
        return pl.ds(pl.multiple_of((x * 4 + place_ref[r]) * BLOCK, BLOCK), BLOCK)

    @pl.when(step == 0)
    def _():
        sums_ref[...] = jnp.zeros_like(sums_ref)

    for piece in range(given):

        @pl.when((step >= piece * taken) & (step < (piece + 1) * taken))
        def _(piece=piece):
            x = [rows[piece][:, columns(step - piece * taken, r)] for r in range(4)]
            for n in range(parts):
                sums_ref[n] += sum(
                    jnp.dot(x[r], ins[r][n], preferred_element_type=F32) for r in range(4)
                )

    @pl.when(step == XS)
    def _():
        for n in range(half):
            g, u = sums_ref[n], sums_ref[half + n]
            hidden_ref[n] = (g / (1.0 + jnp.exp(-g)) * u).astype(BF)

    for x in range(XS):

        @pl.when(step == XS + x)
        def _(x=x):
            for r in range(4):
                made = sum(
                    jnp.dot(hidden_ref[n], downs[r][n], preferred_element_type=F32)
                    for n in range(half)
                )
                outs[x // each][:, columns(x % each, r)] = made.astype(BF)


def expert(place, rows, packs, pieces):
    count = rows[0].shape[0]
    width = sum(r.shape[1] for r in rows)
    half = packs[0].shape[1] // 3
    out = jax.ShapeDtypeStruct((count, width // pieces), BF)
    return pl.pallas_call(
        functools.partial(expert_kernel, len(rows)),
        grid_spec=pltpu.PrefetchScalarGridSpec(
            num_scalar_prefetch=1,
            grid=(2 * XS,),
            in_specs=[pl.BlockSpec(r.shape, lambda s, p: (0, 0)) for r in rows]
            + [
                pl.BlockSpec(
                    (pl.Squeezed(), 2 * half, BLOCK, BLOCK),
                    lambda s, p: (jnp.minimum(s, XS - 1), 0, 0, 0),
                )
            ]
            * 4
            + [
                pl.BlockSpec(
                    (pl.Squeezed(), half, BLOCK, BLOCK),
                    lambda s, p: (jnp.maximum(s - XS, 0), 2, 0, 0),
                )
            ]
            * 4,
            out_specs=[pl.BlockSpec(out.shape, lambda s, p: (0, 0))] * pieces,
            scratch_shapes=[
                pltpu.VMEM((2 * half, count, BLOCK), F32),
                pltpu.VMEM((half, count, BLOCK), BF),
            ],
        ),
        out_shape=[out] * pieces,
        compiler_params=PARAMS,
        name="expert",
    )(place, *rows, *packs, *packs)


def weighted(high_ref, low_ref, i, rows_ref):
    rows = jnp.concatenate([rows_ref[y, i] for y in range(YS)], axis=0)
    return sum(
        lax.dot_general(s[i], rows, (((0,), (0,)), ((), ())), preferred_element_type=F32)
        for s in (high_ref, low_ref)
    )


def pair_kernel(high_ref, low_ref, rows_ref, below_ref, above_ref):
    below_ref[...] = weighted(high_ref, low_ref, 0, rows_ref).astype(BF)
    above_ref[...] = weighted(high_ref, low_ref, 1, rows_ref).astype(BF)


def single_kernel(high_ref, low_ref, rows_ref, out_ref):
    out_ref[...] = weighted(high_ref, low_ref, 0, rows_ref).astype(BF)


def last_kernel(high_ref, low_ref, rows_ref, *refs):
    left, right, far_ref, out_ref = refs[0:2], refs[2:4], refs[4], refs[5]
    total = weighted(high_ref, low_ref, 0, rows_ref) + far_ref[...].astype(F32)
    first = pl.program_id(0) < pl.num_programs(0) // 2

    @pl.when(first)
    def _():
        out_ref[...] = (total + left[0][...].astype(F32) + left[1][...].astype(F32)).astype(BF)

    @pl.when(jnp.logical_not(first))
    def _():
        out_ref[...] = (total + right[0][...].astype(F32) + right[1][...].astype(F32)).astype(BF)


def combine(kernel, plans, rows, first, steps, more, counts):
    _, high, low = plans
    table = pl.BlockSpec(high.shape, lambda j: (0, 0, 0))
    return pl.pallas_call(
        kernel,
        grid=(steps,),
        out_shape=[jax.ShapeDtypeStruct((n, steps * TILE), BF) for n in counts],
        in_specs=[
            table,
            table,
            pl.BlockSpec(rows.shape[:-1] + (TILE,), lambda j: (0, 0, 0, first + j)),
        ]
        + [
            pl.BlockSpec((a.shape[0], TILE), lambda j, n=a.shape[1] // TILE: (0, jnp.minimum(j, n - 1)))
            for a in more
        ],
        out_specs=[pl.BlockSpec((n, TILE), lambda j: (0, j)) for n in counts],
        compiler_params=PARAMS,
        name="combine",
    )(high, low, rows, *more)


def over_y(rows, shape):
    return lax.all_to_all(
        rows.reshape(YS, -1, rows.shape[-1]), "y", split_axis=0, concat_axis=0, tiled=True
    ).reshape(shape)


def on_device(tokens, route_ids, gate_values, w_gate_up, w_down):
    tok_rows, top = route_ids.shape
    model = tokens.shape[1]
    slots = 3 * tok_rows * top // (2 * ZH * YS)
    half = tok_rows // 2
    swap = [(0, 1), (1, 0)]
    group = lax.axis_index("zh").reshape(1)
    barrier = lax.optimization_barrier
    pack = pack_shards(w_gate_up[0], w_down[0])
    meta = jnp.concatenate([route_ids.astype(F32).T, gate_values.T], axis=0)

    pieces = range(model // TILE)
    token_parts = [tokens[:, p * TILE : (p + 1) * TILE] for p in pieces]
    near_metas = [lax.ppermute(meta, "zh", ring(k)) for k in (1, 3)]
    near = [[lax.ppermute(t, "zh", ring(k)) for k in (1, 3)] for t in token_parts]
    swapped = lax.ppermute(pack, "zl", swap)
    mine = lax.all_gather(pack, "x")
    own = plan(group, slots, meta)
    arrived_own = over_y(gather(own[0], [[[tokens]]]), (-1, model))
    sides = plan(group, slots, *near_metas)
    near[0], sides, swapped, arrived_own = barrier((near[0], sides, swapped, arrived_own))
    other = lax.all_gather(swapped, "x")
    far_meta = lax.ppermute(near_metas[0], "zh", ring(1))

    arrived_sides, far = [], []
    for p in pieces:
        arrived_sides.append(over_y(gather(sides[0], [[[t] for t in near[p]]]), (-1, TILE)))
        below, above = near[p]
        far.append(
            [lax.ppermute(below[:half], "zh", ring(1)), lax.ppermute(above[half:], "zh", ring(3))]
        )
        if p == 0:
            near[1], arrived_sides, mine = barrier((near[1], arrived_sides, mine))
            mine_swapped = lax.ppermute(mine, "core", swap)
    across = plan(group, slots, far_meta)
    sent, mine_swapped, arrived_sides, other = barrier(
        (gather(across[0], [[f] for f in far]), mine_swapped, arrived_sides, other)
    )
    arrived_across = over_y(sent, (-1, model))
    packs = [mine, mine_swapped, other, lax.ppermute(other, "core", swap)]
    zl, core = lax.axis_index("zl"), lax.axis_index("core")
    place = jnp.stack([zl * 2 + core, zl * 2 + 1 - core, (1 - zl) * 2 + core, (1 - zl) * 2 + 1 - core])

    made_sides = expert(place, arrived_sides, packs, len(pieces))
    made_sides, arrived_across = barrier((made_sides, arrived_across))
    (made_across,) = expert(place, [arrived_across], packs, 1)
    made_across, arrived_own = barrier((made_across, arrived_own))
    (made_own,) = expert(place, [arrived_own], packs, 1)

    def sums_of_sides(rows):
        below, above = combine(pair_kernel, sides, rows, 0, 1, [], (tok_rows, tok_rows))
        return [lax.ppermute(below, "zh", ring(3)), lax.ppermute(above, "zh", ring(1))]

    left = over_y(made_sides[0], (YS, 2, slots, TILE))
    left, made_across, rows = barrier((left, made_across, made_sides[1]))
    right = over_y(rows, (YS, 2, slots, TILE))
    left_sums = sums_of_sides(left)
    right, made_own, left_sums, made_across = barrier((right, made_own, left_sums, made_across))
    back = over_y(made_across, (YS, 1, slots, model))
    right_sums = sums_of_sides(right)
    (part,) = combine(single_kernel, across, back, 0, len(pieces), [], (tok_rows,))
    made_own, right_sums, part = barrier((made_own, right_sums, part))
    far_sum = lax.ppermute(part, "zh", ring(2))
    back = over_y(made_own, (YS, 1, slots, model))
    home = left_sums + right_sums + [far_sum]
    return combine(last_kernel, own, back, 0, len(pieces), home, (tok_rows,))[0]


def solution(mesh):
    split = Mesh(mesh.devices.reshape(ZH, YS, XS, 2, 2), ("zh", "y", "x", "zl", "core"))
    owner, shard = ("zh", "y"), ("x", "zl", "core")
    every = owner + shard
    in_specs = (P(every, None),) * 3 + (P(owner, shard, None), P(owner, None, shard))
    return jax.shard_map(
        on_device, mesh=split, in_specs=in_specs, out_specs=P(every, None), check_vma=False
    )
```

```python
import functools

import jax
import jax.numpy as jnp
from jax import lax
from jax.experimental import pallas as pl
from jax.experimental.pallas import tpu as pltpu
from jax.sharding import Mesh, PartitionSpec as P

BF, F32 = jnp.bfloat16, jnp.float32
ZH, YS, XS = 4, 4, 4
PARAMS = pltpu.CompilerParams(vmem_limit_bytes=56 << 20)
BLOCK = 256
TILE = 2048


def ring(step):
    return [(i, (i + step) % ZH) for i in range(ZH)]


def pack_kernel(up_ref, down_ref, out_ref):
    step = pl.program_id(0)

    @pl.when(step < 2)
    def _():
        for n in range(3):
            out_ref[n] = up_ref[:, n * BLOCK : (n + 1) * BLOCK]

    @pl.when(step == 2)
    def _():
        for n in range(3):
            out_ref[n] = down_ref[n * BLOCK : (n + 1) * BLOCK, :]


def pack_shards(up, down):
    return pl.pallas_call(
        pack_kernel,
        grid=(3,),
        out_shape=jax.ShapeDtypeStruct((9, BLOCK, BLOCK), BF),
        in_specs=[
            pl.BlockSpec((BLOCK, 3 * BLOCK), lambda s: (0, jnp.minimum(s, 1))),
            pl.BlockSpec((3 * BLOCK, BLOCK), lambda s: (0, 0)),
        ],
        out_specs=pl.BlockSpec((3, BLOCK, BLOCK), lambda s: (s, 0, 0)),
        compiler_params=PARAMS,
        name="pack",
    )(up, down)


def plan_kernel(group_ref, *refs):
    metas, (pick_ref, high_ref, low_ref) = refs[:-3], refs[-3:]
    rows = metas[0].shape[1]
    slots = pick_ref.shape[1] // YS
    group = group_ref[0]
    named, gates = [], []
    for meta_ref in metas:
        ids, weights = meta_ref[0:4, :], meta_ref[4:8, :]
        for y in range(YS):
            match = ids == (group * YS + y).astype(F32)
            named.append(jnp.sum(match.astype(F32), axis=0, keepdims=True))
            gates.append(jnp.sum(jnp.where(match, weights, 0.0), axis=0, keepdims=True))
    stacked = jnp.concatenate(named, axis=0)
    earlier = lax.broadcasted_iota(jnp.int32, (rows, rows), 0)
    later = lax.broadcasted_iota(jnp.int32, (rows, rows), 1)
    rank = jnp.dot(
        stacked.astype(BF), (earlier < later).astype(F32).astype(BF), preferred_element_type=F32
    )
    slot = lax.broadcasted_iota(jnp.int32, (slots, rows), 0).astype(F32)
    for k in range(len(metas)):
        for y in range(YS):
            i = k * YS + y
            here = (rank[i : i + 1, :] == slot) & (named[i] > 0.5)
            at = slice(y * slots, (y + 1) * slots)
            scaled = jnp.where(here, gates[i], 0.0)
            high = scaled.astype(BF)
            pick_ref[k, at, :] = here.astype(F32).astype(BF)
            high_ref[k, at, :] = high
            low_ref[k, at, :] = (scaled - high.astype(F32)).astype(BF)


def plan(group, slots, *metas):
    out = jax.ShapeDtypeStruct((len(metas), YS * slots, metas[0].shape[1]), BF)
    return pl.pallas_call(
        plan_kernel,
        out_shape=(out, out, out),
        in_specs=[pl.BlockSpec(memory_space=pltpu.SMEM)] + [pl.BlockSpec()] * len(metas),
        compiler_params=PARAMS,
        name="plan",
    )(group, *metas)


def gather_kernel(pieces, pick_ref, *refs):
    blocks, out_ref = refs[:-1], refs[-1]
    slots = out_ref.shape[2]
    for i in range(pick_ref.shape[0]):
        rows = jnp.concatenate([ref[...] for ref in blocks[i * pieces : (i + 1) * pieces]], axis=0)
        got = jnp.dot(pick_ref[i], rows, preferred_element_type=F32).astype(BF)
        for y in range(YS):
            out_ref[y, i] = got[y * slots : (y + 1) * slots]


def gather(pick, *blocks):
    sources, routes, _ = pick.shape
    width = blocks[0].shape[1]
    shape = (YS, sources, routes // YS)
    return pl.pallas_call(
        functools.partial(gather_kernel, len(blocks) // sources),
        grid=(width // TILE,),
        out_shape=jax.ShapeDtypeStruct(shape + (width,), BF),
        in_specs=[pl.BlockSpec(pick.shape, lambda j: (0, 0, 0))]
        + [pl.BlockSpec((b.shape[0], TILE), lambda j: (0, j)) for b in blocks],
        out_specs=pl.BlockSpec(shape + (TILE,), lambda j: (0, 0, 0, j)),
        compiler_params=PARAMS,
        name="gather",
    )(pick, *blocks)


def expert_kernel(place_ref, x_ref, *refs):
    ins, downs, outs = refs[0:4], refs[4:8], refs[8:-2]
    sums_ref, hidden_ref = refs[-2:]
    step = pl.program_id(0)
    parts = sums_ref.shape[0]
    half = parts // 2
    each = XS // len(outs)

    def columns(x, r):
        return pl.ds(pl.multiple_of((x * 4 + place_ref[r]) * BLOCK, BLOCK), BLOCK)

    @pl.when(step == 0)
    def _():
        sums_ref[...] = jnp.zeros_like(sums_ref)

    @pl.when(step < XS)
    def _():
        rows = [x_ref[:, columns(step, r)] for r in range(4)]
        for n in range(parts):
            sums_ref[n] += sum(
                jnp.dot(rows[r], ins[r][n], preferred_element_type=F32) for r in range(4)
            )

    @pl.when(step == XS)
    def _():
        for n in range(half):
            g, u = sums_ref[n], sums_ref[half + n]
            hidden_ref[n] = (g / (1.0 + jnp.exp(-g)) * u).astype(BF)

    for x in range(XS):

        @pl.when(step == XS + x)
        def _(x=x):
            for r in range(4):
                made = sum(
                    jnp.dot(hidden_ref[n], downs[r][n], preferred_element_type=F32)
                    for n in range(half)
                )
                outs[x // each][:, columns(x % each, r)] = made.astype(BF)


def expert(place, rows, packs, pieces):
    count, width = rows.shape
    half = packs[0].shape[1] // 3
    out = jax.ShapeDtypeStruct((count, width // pieces), BF)
    return pl.pallas_call(
        expert_kernel,
        grid_spec=pltpu.PrefetchScalarGridSpec(
            num_scalar_prefetch=1,
            grid=(2 * XS,),
            in_specs=[pl.BlockSpec((count, width), lambda s, p: (0, 0))]
            + [
                pl.BlockSpec(
                    (pl.Squeezed(), 2 * half, BLOCK, BLOCK),
                    lambda s, p: (jnp.minimum(s, XS - 1), 0, 0, 0),
                )
            ]
            * 4
            + [
                pl.BlockSpec(
                    (pl.Squeezed(), half, BLOCK, BLOCK),
                    lambda s, p: (jnp.maximum(s - XS, 0), 2, 0, 0),
                )
            ]
            * 4,
            out_specs=[pl.BlockSpec(out.shape, lambda s, p: (0, 0))] * pieces,
            scratch_shapes=[
                pltpu.VMEM((2 * half, count, BLOCK), F32),
                pltpu.VMEM((half, count, BLOCK), BF),
            ],
        ),
        out_shape=[out] * pieces,
        compiler_params=PARAMS,
        name="expert",
    )(place, rows, *packs, *packs)


def weighted(high_ref, low_ref, i, rows_ref):
    rows = jnp.concatenate([rows_ref[y, i] for y in range(YS)], axis=0)
    return sum(
        lax.dot_general(s[i], rows, (((0,), (0,)), ((), ())), preferred_element_type=F32)
        for s in (high_ref, low_ref)
    )


def split_kernel(high_ref, low_ref, rows_ref, top_ref, bottom_ref):
    total = weighted(high_ref, low_ref, 0, rows_ref).astype(BF)
    half = top_ref.shape[0]
    top_ref[...], bottom_ref[...] = total[:half], total[half:]


def add_kernel(high_ref, low_ref, rows_ref, top_ref, bottom_ref, below_ref, above_ref):
    half = top_ref.shape[0]
    below = weighted(high_ref, low_ref, 0, rows_ref)
    above = weighted(high_ref, low_ref, 1, rows_ref)
    below_ref[:half, :] = (below[:half] + top_ref[...].astype(F32)).astype(BF)
    below_ref[half:, :] = below[half:].astype(BF)
    above_ref[:half, :] = above[:half].astype(BF)
    above_ref[half:, :] = (above[half:] + bottom_ref[...].astype(F32)).astype(BF)


def pair_kernel(high_ref, low_ref, rows_ref, below_ref, above_ref):
    below_ref[...] = weighted(high_ref, low_ref, 0, rows_ref).astype(BF)
    above_ref[...] = weighted(high_ref, low_ref, 1, rows_ref).astype(BF)


def single_kernel(high_ref, low_ref, rows_ref, out_ref):
    out_ref[...] = weighted(high_ref, low_ref, 0, rows_ref).astype(BF)


def last_kernel(high_ref, low_ref, rows_ref, *refs):
    left, right, out_ref = refs[0:3], refs[3:5], refs[5]
    total = weighted(high_ref, low_ref, 0, rows_ref)
    first = pl.program_id(0) == 0

    @pl.when(first)
    def _():
        out_ref[...] = sum([ref[...].astype(F32) for ref in left], total).astype(BF)

    @pl.when(jnp.logical_not(first))
    def _():
        out_ref[...] = sum([ref[...].astype(F32) for ref in right], total).astype(BF)


def combine(kernel, plans, rows, first, steps, more, counts):
    _, high, low = plans
    table = pl.BlockSpec(high.shape, lambda j: (0, 0, 0))
    return pl.pallas_call(
        kernel,
        grid=(steps,),
        out_shape=[jax.ShapeDtypeStruct((n, steps * TILE), BF) for n in counts],
        in_specs=[
            table,
            table,
            pl.BlockSpec(rows.shape[:-1] + (TILE,), lambda j: (0, 0, 0, first + j)),
        ]
        + [pl.BlockSpec(a.shape, lambda j: (0, 0)) for a in more],
        out_specs=[pl.BlockSpec((n, TILE), lambda j: (0, j)) for n in counts],
        compiler_params=PARAMS,
        name="combine",
    )(high, low, rows, *more)


def over_y(rows, shape):
    return lax.all_to_all(
        rows.reshape(YS, -1, rows.shape[-1]), "y", split_axis=0, concat_axis=0, tiled=True
    ).reshape(shape)


def on_device(tokens, route_ids, gate_values, w_gate_up, w_down):
    tok_rows, top = route_ids.shape
    model = tokens.shape[1]
    slots = 3 * tok_rows * top // (2 * ZH * YS)
    half = tok_rows // 2
    swap = [(0, 1), (1, 0)]
    group = lax.axis_index("zh").reshape(1)
    barrier = lax.optimization_barrier
    pack = pack_shards(w_gate_up[0], w_down[0])
    meta = jnp.concatenate([route_ids.astype(F32).T, gate_values.T], axis=0)

    near = [lax.ppermute(tokens, "zh", ring(k)) for k in (1, 3)]
    near_metas = [lax.ppermute(meta, "zh", ring(k)) for k in (1, 3)]
    swapped = lax.ppermute(pack, "zl", swap)
    mine = lax.all_gather(pack, "x")
    own = plan(group, slots, meta)
    arrived_own = over_y(gather(own[0], tokens), (-1, model))
    sides = plan(group, slots, *near_metas)
    near, sides, swapped, arrived_own = barrier((near, sides, swapped, arrived_own))
    other = lax.all_gather(swapped, "x")

    arrived_sides = over_y(gather(sides[0], *near), (-1, model))
    far = [lax.ppermute(near[0][:half], "zh", ring(1)), lax.ppermute(near[1][half:], "zh", ring(3))]
    far_meta = lax.ppermute(near_metas[0], "zh", ring(1))
    across = plan(group, slots, far_meta)
    sent, mine, arrived_sides = barrier((gather(across[0], *far), mine, arrived_sides))
    mine_swapped = lax.ppermute(mine, "core", swap)
    arrived_across = over_y(sent, (-1, model))
    packs = [mine, mine_swapped, other, lax.ppermute(other, "core", swap)]
    zl, core = lax.axis_index("zl"), lax.axis_index("core")
    place = jnp.stack([zl * 2 + core, zl * 2 + 1 - core, (1 - zl) * 2 + core, (1 - zl) * 2 + 1 - core])

    made_sides = expert(place, arrived_sides, packs, 2)
    made_sides, arrived_across = barrier((made_sides, arrived_across))
    (made,) = expert(place, arrived_across, packs, 1)
    made, arrived_own = barrier((made, arrived_own))
    (made_own,) = expert(place, arrived_own, packs, 1)

    left = over_y(made_sides[0], (YS, 2, slots, TILE))
    left, made = barrier((left, made))
    back = over_y(made, (YS, 1, slots, model))
    below, above = combine(pair_kernel, sides, left, 0, 1, [], (tok_rows, tok_rows))
    home = [lax.ppermute(below, "zh", ring(3)), lax.ppermute(above, "zh", ring(1))]
    back, made_own = barrier((back, made_own))
    top, bottom = combine(split_kernel, across, back, 1, 1, [], (half, half))
    (straight,) = combine(single_kernel, across, back, 0, 1, [], (tok_rows,))
    rows, top, bottom, straight, home = barrier((made_sides[1], top, bottom, straight, home))
    passed = [lax.ppermute(top, "zh", ring(3)), lax.ppermute(bottom, "zh", ring(1))]
    straight = lax.ppermute(straight, "zh", ring(2))
    right = over_y(rows, (YS, 2, slots, TILE))
    below, above = combine(add_kernel, sides, right, 0, 1, passed, (tok_rows, tok_rows))
    made_own, below, above, straight = barrier((made_own, below, above, straight))
    home = home + [straight, lax.ppermute(below, "zh", ring(3)), lax.ppermute(above, "zh", ring(1))]
    back = over_y(made_own, (YS, 1, slots, model))
    return combine(last_kernel, own, back, 0, 2, home, (tok_rows,))[0]


def solution(mesh):
    split = Mesh(mesh.devices.reshape(ZH, YS, XS, 2, 2), ("zh", "y", "x", "zl", "core"))
    owner, shard = ("zh", "y"), ("x", "zl", "core")
    every = owner + shard
    in_specs = (P(every, None),) * 3 + (P(owner, shard, None), P(owner, None, shard))
    return jax.shard_map(
        on_device, mesh=split, in_specs=in_specs, out_specs=P(every, None), check_vma=False
    )
```

```python
import functools

import jax
import jax.numpy as jnp
from jax import lax
from jax.experimental import pallas as pl
from jax.experimental.pallas import tpu as pltpu
from jax.sharding import Mesh, PartitionSpec as P

BF, F32 = jnp.bfloat16, jnp.float32
ZH, YS, XS = 4, 4, 4
PARAMS = pltpu.CompilerParams(vmem_limit_bytes=56 << 20)
BLOCK = 256
TILE = 2048


def ring(step):
    return [(i, (i + step) % ZH) for i in range(ZH)]


def pack_kernel(up_ref, down_ref, out_ref):
    step = pl.program_id(0)

    @pl.when(step < 2)
    def _():
        for n in range(3):
            out_ref[n] = up_ref[:, n * BLOCK : (n + 1) * BLOCK]

    @pl.when(step == 2)
    def _():
        for n in range(3):
            out_ref[n] = down_ref[n * BLOCK : (n + 1) * BLOCK, :]


def pack_shards(up, down):
    return pl.pallas_call(
        pack_kernel,
        grid=(3,),
        out_shape=jax.ShapeDtypeStruct((9, BLOCK, BLOCK), BF),
        in_specs=[
            pl.BlockSpec((BLOCK, 3 * BLOCK), lambda s: (0, jnp.minimum(s, 1))),
            pl.BlockSpec((3 * BLOCK, BLOCK), lambda s: (0, 0)),
        ],
        out_specs=pl.BlockSpec((3, BLOCK, BLOCK), lambda s: (s, 0, 0)),
        compiler_params=PARAMS,
        name="pack",
    )(up, down)


def plan_kernel(group_ref, *refs):
    metas, (pick_ref, high_ref, low_ref) = refs[:-3], refs[-3:]
    rows = metas[0].shape[1]
    slots = pick_ref.shape[1] // YS
    group = group_ref[0]
    named, gates = [], []
    for meta_ref in metas:
        ids, weights = meta_ref[0:4, :], meta_ref[4:8, :]
        for y in range(YS):
            match = ids == (group * YS + y).astype(F32)
            named.append(jnp.sum(match.astype(F32), axis=0, keepdims=True))
            gates.append(jnp.sum(jnp.where(match, weights, 0.0), axis=0, keepdims=True))
    stacked = jnp.concatenate(named, axis=0)
    earlier = lax.broadcasted_iota(jnp.int32, (rows, rows), 0)
    later = lax.broadcasted_iota(jnp.int32, (rows, rows), 1)
    rank = jnp.dot(
        stacked.astype(BF), (earlier < later).astype(F32).astype(BF), preferred_element_type=F32
    )
    slot = lax.broadcasted_iota(jnp.int32, (slots, rows), 0).astype(F32)
    for k in range(len(metas)):
        for y in range(YS):
            i = k * YS + y
            here = (rank[i : i + 1, :] == slot) & (named[i] > 0.5)
            at = slice(y * slots, (y + 1) * slots)
            scaled = jnp.where(here, gates[i], 0.0)
            high = scaled.astype(BF)
            pick_ref[k, at, :] = here.astype(F32).astype(BF)
            high_ref[k, at, :] = high
            low_ref[k, at, :] = (scaled - high.astype(F32)).astype(BF)


def plan(group, slots, *metas):
    out = jax.ShapeDtypeStruct((len(metas), YS * slots, metas[0].shape[1]), BF)
    return pl.pallas_call(
        plan_kernel,
        out_shape=(out, out, out),
        in_specs=[pl.BlockSpec(memory_space=pltpu.SMEM)] + [pl.BlockSpec()] * len(metas),
        compiler_params=PARAMS,
        name="plan",
    )(group, *metas)


def gather_kernel(pieces, pick_ref, *refs):
    blocks, out_ref = refs[:-1], refs[-1]
    slots = out_ref.shape[2]
    for i in range(pick_ref.shape[0]):
        rows = jnp.concatenate([ref[...] for ref in blocks[i * pieces : (i + 1) * pieces]], axis=0)
        got = jnp.dot(pick_ref[i], rows, preferred_element_type=F32).astype(BF)
        for y in range(YS):
            out_ref[y, i] = got[y * slots : (y + 1) * slots]


def gather(pick, *blocks):
    sources, routes, _ = pick.shape
    width = blocks[0].shape[1]
    shape = (YS, sources, routes // YS)
    return pl.pallas_call(
        functools.partial(gather_kernel, len(blocks) // sources),
        grid=(width // TILE,),
        out_shape=jax.ShapeDtypeStruct(shape + (width,), BF),
        in_specs=[pl.BlockSpec(pick.shape, lambda j: (0, 0, 0))]
        + [pl.BlockSpec((b.shape[0], TILE), lambda j: (0, j)) for b in blocks],
        out_specs=pl.BlockSpec(shape + (TILE,), lambda j: (0, 0, 0, j)),
        compiler_params=PARAMS,
        name="gather",
    )(pick, *blocks)


def expert_kernel(place_ref, x_ref, *refs):
    ins, downs, outs = refs[0:4], refs[4:8], refs[8:-2]
    sums_ref, hidden_ref = refs[-2:]
    step = pl.program_id(0)
    parts = sums_ref.shape[0]
    half = parts // 2
    each = XS // len(outs)

    def columns(x, r):
        return pl.ds(pl.multiple_of((x * 4 + place_ref[r]) * BLOCK, BLOCK), BLOCK)

    @pl.when(step == 0)
    def _():
        sums_ref[...] = jnp.zeros_like(sums_ref)

    @pl.when(step < XS)
    def _():
        rows = [x_ref[:, columns(step, r)] for r in range(4)]
        for n in range(parts):
            sums_ref[n] += sum(
                jnp.dot(rows[r], ins[r][n], preferred_element_type=F32) for r in range(4)
            )

    @pl.when(step == XS)
    def _():
        for n in range(half):
            g, u = sums_ref[n], sums_ref[half + n]
            hidden_ref[n] = (g / (1.0 + jnp.exp(-g)) * u).astype(BF)

    for x in range(XS):

        @pl.when(step == XS + x)
        def _(x=x):
            for r in range(4):
                made = sum(
                    jnp.dot(hidden_ref[n], downs[r][n], preferred_element_type=F32)
                    for n in range(half)
                )
                outs[x // each][:, columns(x % each, r)] = made.astype(BF)


def expert(place, rows, packs, pieces):
    count, width = rows.shape
    half = packs[0].shape[1] // 3
    out = jax.ShapeDtypeStruct((count, width // pieces), BF)
    return pl.pallas_call(
        expert_kernel,
        grid_spec=pltpu.PrefetchScalarGridSpec(
            num_scalar_prefetch=1,
            grid=(2 * XS,),
            in_specs=[pl.BlockSpec((count, width), lambda s, p: (0, 0))]
            + [
                pl.BlockSpec(
                    (pl.Squeezed(), 2 * half, BLOCK, BLOCK),
                    lambda s, p: (jnp.minimum(s, XS - 1), 0, 0, 0),
                )
            ]
            * 4
            + [
                pl.BlockSpec(
                    (pl.Squeezed(), half, BLOCK, BLOCK),
                    lambda s, p: (jnp.maximum(s - XS, 0), 2, 0, 0),
                )
            ]
            * 4,
            out_specs=[pl.BlockSpec(out.shape, lambda s, p: (0, 0))] * pieces,
            scratch_shapes=[
                pltpu.VMEM((2 * half, count, BLOCK), F32),
                pltpu.VMEM((half, count, BLOCK), BF),
            ],
        ),
        out_shape=[out] * pieces,
        compiler_params=PARAMS,
        name="expert",
    )(place, rows, *packs, *packs)


def weighted(high_ref, low_ref, i, rows_ref):
    rows = jnp.concatenate([rows_ref[y, i] for y in range(YS)], axis=0)
    return sum(
        lax.dot_general(s[i], rows, (((0,), (0,)), ((), ())), preferred_element_type=F32)
        for s in (high_ref, low_ref)
    )


def split_kernel(high_ref, low_ref, rows_ref, top_ref, bottom_ref):
    total = weighted(high_ref, low_ref, 0, rows_ref).astype(BF)
    half = top_ref.shape[0]
    top_ref[...], bottom_ref[...] = total[:half], total[half:]


def add_kernel(high_ref, low_ref, rows_ref, top_ref, bottom_ref, below_ref, above_ref):
    half = top_ref.shape[0]
    below = weighted(high_ref, low_ref, 0, rows_ref)
    above = weighted(high_ref, low_ref, 1, rows_ref)
    below_ref[:half, :] = (below[:half] + top_ref[...].astype(F32)).astype(BF)
    below_ref[half:, :] = below[half:].astype(BF)
    above_ref[:half, :] = above[:half].astype(BF)
    above_ref[half:, :] = (above[half:] + bottom_ref[...].astype(F32)).astype(BF)


def last_kernel(high_ref, low_ref, rows_ref, *refs):
    left, right, out_ref = refs[0:2], refs[2:4], refs[4]
    total = weighted(high_ref, low_ref, 0, rows_ref)
    first = pl.program_id(0) < pl.num_programs(0) // 2

    @pl.when(first)
    def _():
        out_ref[...] = (total + left[0][...].astype(F32) + left[1][...].astype(F32)).astype(BF)

    @pl.when(jnp.logical_not(first))
    def _():
        out_ref[...] = (total + right[0][...].astype(F32) + right[1][...].astype(F32)).astype(BF)


def combine(kernel, plans, rows, first, steps, more, counts):
    _, high, low = plans
    table = pl.BlockSpec(high.shape, lambda j: (0, 0, 0))
    return pl.pallas_call(
        kernel,
        grid=(steps,),
        out_shape=[jax.ShapeDtypeStruct((n, steps * TILE), BF) for n in counts],
        in_specs=[
            table,
            table,
            pl.BlockSpec(rows.shape[:-1] + (TILE,), lambda j: (0, 0, 0, first + j)),
        ]
        + [pl.BlockSpec(a.shape, lambda j: (0, 0)) for a in more],
        out_specs=[pl.BlockSpec((n, TILE), lambda j: (0, j)) for n in counts],
        compiler_params=PARAMS,
        name="combine",
    )(high, low, rows, *more)


def over_y(rows, shape):
    return lax.all_to_all(
        rows.reshape(YS, -1, rows.shape[-1]), "y", split_axis=0, concat_axis=0, tiled=True
    ).reshape(shape)


def on_device(tokens, route_ids, gate_values, w_gate_up, w_down):
    tok_rows, top = route_ids.shape
    model = tokens.shape[1]
    slots = 3 * tok_rows * top // (2 * ZH * YS)
    half = tok_rows // 2
    swap = [(0, 1), (1, 0)]
    group = lax.axis_index("zh").reshape(1)
    barrier = lax.optimization_barrier
    pack = pack_shards(w_gate_up[0], w_down[0])
    meta = jnp.concatenate([route_ids.astype(F32).T, gate_values.T], axis=0)

    near_metas = [lax.ppermute(meta, "zh", ring(k)) for k in (1, 3)]
    far_meta = lax.ppermute(meta, "zh", ring(2))
    swapped = lax.ppermute(pack, "zl", swap)
    mine = lax.all_gather(pack, "x")
    own = plan(group, slots, meta)
    sent = gather(own[0], tokens)
    sides = plan(group, slots, *near_metas)
    across = plan(group, slots, far_meta)
    swapped, sent, sides, across, moved = barrier((swapped, sent, sides, across, tokens))
    other = lax.all_gather(swapped, "x")
    arrived_own = over_y(sent, (-1, model))
    near = [lax.ppermute(moved, "zh", ring(k)) for k in (1, 3)]
    near, arrived_own = barrier((near, arrived_own))

    arrived_sides = over_y(gather(sides[0], *near), (-1, model))
    far = [lax.ppermute(near[0][:half], "zh", ring(1)), lax.ppermute(near[1][half:], "zh", ring(3))]
    sent, mine, arrived_sides = barrier((gather(across[0], *far), mine, arrived_sides))
    mine_swapped = lax.ppermute(mine, "core", swap)
    arrived_across = over_y(sent, (-1, model))
    packs = [mine, mine_swapped, other, lax.ppermute(other, "core", swap)]
    zl, core = lax.axis_index("zl"), lax.axis_index("core")
    place = jnp.stack([zl * 2 + core, zl * 2 + 1 - core, (1 - zl) * 2 + core, (1 - zl) * 2 + 1 - core])

    made_sides = expert(place, arrived_sides, packs, 2)
    made_sides, arrived_across = barrier((made_sides, arrived_across))
    (made,) = expert(place, arrived_across, packs, 1)

    back = over_y(made, (YS, 1, slots, model))
    pieces = range(model // TILE)
    parts = [combine(split_kernel, across, back, p, 1, [], (half, half)) for p in pieces]
    passed = [
        [lax.ppermute(top, "zh", ring(3)), lax.ppermute(bottom, "zh", ring(1))] for top, bottom in parts
    ]
    arrived_own, parts = barrier((arrived_own, parts))
    (made_own,) = expert(place, arrived_own, packs, 1)
    home, rows = [], made_sides[0]
    for p in pieces:
        rows, back = barrier((rows, back))
        back = over_y(rows, (YS, 2, slots, TILE))
        if p == 0:
            rows, passed[0], made_own = barrier((made_sides[1], passed[0], made_own))
            back, passed[1] = barrier((back, passed[1]))
        below, above = combine(add_kernel, sides, back, 0, 1, passed[p], (tok_rows, tok_rows))
        if p == 1:
            made_own, home, below, above = barrier((made_own, home, below, above))
        home = home + [lax.ppermute(below, "zh", ring(3)), lax.ppermute(above, "zh", ring(1))]
    back = over_y(made_own, (YS, 1, slots, model))
    return combine(last_kernel, own, back, 0, len(pieces), home, (tok_rows,))[0]


def solution(mesh):
    split = Mesh(mesh.devices.reshape(ZH, YS, XS, 2, 2), ("zh", "y", "x", "zl", "core"))
    owner, shard = ("zh", "y"), ("x", "zl", "core")
    every = owner + shard
    in_specs = (P(every, None),) * 3 + (P(owner, shard, None), P(owner, None, shard))
    return jax.shard_map(
        on_device, mesh=split, in_specs=in_specs, out_specs=P(every, None), check_vma=False
    )
```

```python
import functools

import jax
import jax.numpy as jnp
from jax import lax
from jax.experimental import pallas as pl
from jax.experimental.pallas import tpu as pltpu
from jax.sharding import Mesh, PartitionSpec as P

BF, F32 = jnp.bfloat16, jnp.float32
ZH, YS, XS = 4, 4, 4
PARAMS = pltpu.CompilerParams(vmem_limit_bytes=56 << 20)
BLOCK = 256
AHEAD = 3
TILE = 2048


def ring(step):
    return [(i, (i + step) % ZH) for i in range(ZH)]


def pack_kernel(up_ref, down_ref, out_ref):
    step = pl.program_id(0)

    @pl.when(step < 2)
    def _():
        for n in range(3):
            out_ref[n] = up_ref[:, n * BLOCK : (n + 1) * BLOCK]

    @pl.when(step == 2)
    def _():
        for n in range(3):
            out_ref[n] = down_ref[n * BLOCK : (n + 1) * BLOCK, :]


def pack_shards(up, down):
    return pl.pallas_call(
        pack_kernel,
        grid=(3,),
        out_shape=jax.ShapeDtypeStruct((9, BLOCK, BLOCK), BF),
        in_specs=[
            pl.BlockSpec((BLOCK, 3 * BLOCK), lambda s: (0, jnp.minimum(s, 1))),
            pl.BlockSpec((3 * BLOCK, BLOCK), lambda s: (0, 0)),
        ],
        out_specs=pl.BlockSpec((3, BLOCK, BLOCK), lambda s: (s, 0, 0)),
        compiler_params=PARAMS,
        name="pack",
    )(up, down)


def plan_kernel(group_ref, *refs):
    metas, (pick_ref, high_ref, low_ref) = refs[:-3], refs[-3:]
    rows = metas[0].shape[1]
    slots = pick_ref.shape[1] // YS
    group = group_ref[0]
    named, gates = [], []
    for meta_ref in metas:
        ids, weights = meta_ref[0:4, :], meta_ref[4:8, :]
        for y in range(YS):
            match = ids == (group * YS + y).astype(F32)
            named.append(jnp.sum(match.astype(F32), axis=0, keepdims=True))
            gates.append(jnp.sum(jnp.where(match, weights, 0.0), axis=0, keepdims=True))
    stacked = jnp.concatenate(named, axis=0)
    earlier = lax.broadcasted_iota(jnp.int32, (rows, rows), 0)
    later = lax.broadcasted_iota(jnp.int32, (rows, rows), 1)
    rank = jnp.dot(
        stacked.astype(BF), (earlier < later).astype(F32).astype(BF), preferred_element_type=F32
    )
    slot = lax.broadcasted_iota(jnp.int32, (slots, rows), 0).astype(F32)
    for k in range(len(metas)):
        for y in range(YS):
            i = k * YS + y
            here = (rank[i : i + 1, :] == slot) & (named[i] > 0.5)
            at = slice(y * slots, (y + 1) * slots)
            scaled = jnp.where(here, gates[i], 0.0)
            high = scaled.astype(BF)
            pick_ref[k, at, :] = here.astype(F32).astype(BF)
            high_ref[k, at, :] = high
            low_ref[k, at, :] = (scaled - high.astype(F32)).astype(BF)


def plan(group, slots, *metas):
    out = jax.ShapeDtypeStruct((len(metas), YS * slots, metas[0].shape[1]), BF)
    return pl.pallas_call(
        plan_kernel,
        out_shape=(out, out, out),
        in_specs=[pl.BlockSpec(memory_space=pltpu.SMEM)] + [pl.BlockSpec()] * len(metas),
        compiler_params=PARAMS,
        name="plan",
    )(group, *metas)


def gather_kernel(pieces, pick_ref, *refs):
    blocks, out_ref = refs[:-1], refs[-1]
    slots = out_ref.shape[2]
    for i in range(pick_ref.shape[0]):
        rows = jnp.concatenate([ref[...] for ref in blocks[i * pieces : (i + 1) * pieces]], axis=0)
        got = jnp.dot(pick_ref[i], rows, preferred_element_type=F32).astype(BF)
        for y in range(YS):
            out_ref[y, i] = got[y * slots : (y + 1) * slots]


def gather(pick, *blocks):
    sources, routes, _ = pick.shape
    width = blocks[0].shape[1]
    shape = (YS, sources, routes // YS)
    return pl.pallas_call(
        functools.partial(gather_kernel, len(blocks) // sources),
        grid=(width // TILE,),
        out_shape=jax.ShapeDtypeStruct(shape + (width,), BF),
        in_specs=[pl.BlockSpec(pick.shape, lambda j: (0, 0, 0))]
        + [pl.BlockSpec((b.shape[0], TILE), lambda j: (0, j)) for b in blocks],
        out_specs=pl.BlockSpec(shape + (TILE,), lambda j: (0, 0, 0, j)),
        compiler_params=PARAMS,
        name="gather",
    )(pick, *blocks)


def expert_kernel(pieces, place_ref, x_hbm, *refs):
    packs, outs = refs[:4], refs[4 : 4 + pieces]
    x_ref, w_ref, sums_ref, hidden_ref, out_ref, x_sem, in_sems, down_sems, out_sems = refs[4 + pieces :]
    parts = sums_ref.shape[0]
    half = parts // 2
    wide = 4 * BLOCK

    def copy_in(r, x):
        return pltpu.make_async_copy(
            packs[r].at[x, pl.ds(0, parts)], w_ref.at[r, x, pl.ds(0, parts)], in_sems.at[r, x]
        )

    def copy_down(r, x):
        return pltpu.make_async_copy(
            packs[r].at[x, pl.ds(parts, half)], w_ref.at[r, x, pl.ds(parts, half)], down_sems.at[r, x]
        )

    def copy_out(x):
        at = x % (XS // pieces) * wide
        return pltpu.make_async_copy(
            out_ref.at[:, pl.ds(x * wide, wide)],
            outs[x // (XS // pieces)].at[:, pl.ds(at, wide)],
            out_sems.at[x],
        )

    def columns(x, r):
        return pl.ds(pl.multiple_of((x * 4 + place_ref[r]) * BLOCK, BLOCK), BLOCK)

    rows = pltpu.make_async_copy(x_hbm, x_ref, x_sem)
    rows.start()
    order = [(copy, x) for copy in (copy_in, copy_down) for x in range(XS)]

    def start(i):
        if i < len(order):
            copy, x = order[i]
            for r in range(4):
                copy(r, x).start()

    for i in range(AHEAD):
        start(i)
    sums_ref[...] = jnp.zeros_like(sums_ref)
    rows.wait()
    for x in range(XS):
        for r in range(4):
            copy_in(r, x).wait()
        start(x + AHEAD)
        taken = [x_ref[:, columns(x, r)] for r in range(4)]
        for n in range(parts):
            sums_ref[n] += sum(
                jnp.dot(taken[r], w_ref[r, x, n], preferred_element_type=F32) for r in range(4)
            )
    for n in range(half):
        g, u = sums_ref[n], sums_ref[half + n]
        hidden_ref[n] = (g / (1.0 + jnp.exp(-g)) * u).astype(BF)
    for x in range(XS):
        for r in range(4):
            copy_down(r, x).wait()
        start(XS + x + AHEAD)
        for r in range(4):
            made = sum(
                jnp.dot(hidden_ref[n], w_ref[r, x, parts + n], preferred_element_type=F32)
                for n in range(half)
            )
            out_ref[:, columns(x, r)] = made.astype(BF)
        copy_out(x).start()
    for x in range(XS):
        copy_out(x).wait()


def expert(place, rows, packs, pieces):
    count, width = rows.shape
    total = packs[0].shape[1]
    half = total // 3
    out = jax.ShapeDtypeStruct((count, width // pieces), BF)
    there = pl.BlockSpec(memory_space=pl.ANY)
    return pl.pallas_call(
        functools.partial(expert_kernel, pieces),
        in_specs=[pl.BlockSpec(memory_space=pltpu.SMEM)] + [there] * 5,
        out_specs=[there] * pieces,
        out_shape=[out] * pieces,
        scratch_shapes=[
            pltpu.VMEM((count, width), BF),
            pltpu.VMEM((4,) + packs[0].shape, BF),
            pltpu.VMEM((2 * half, count, BLOCK), F32),
            pltpu.VMEM((half, count, BLOCK), BF),
            pltpu.VMEM((count, width), BF),
            pltpu.SemaphoreType.DMA(()),
            pltpu.SemaphoreType.DMA((4, XS)),
            pltpu.SemaphoreType.DMA((4, XS)),
            pltpu.SemaphoreType.DMA((XS,)),
        ],
        compiler_params=PARAMS,
        name="expert",
    )(place, rows, *packs)


def weighted(high_ref, low_ref, i, rows_ref):
    rows = jnp.concatenate([rows_ref[y, i] for y in range(YS)], axis=0)
    return sum(
        lax.dot_general(s[i], rows, (((0,), (0,)), ((), ())), preferred_element_type=F32)
        for s in (high_ref, low_ref)
    )


def split_kernel(high_ref, low_ref, rows_ref, top_ref, bottom_ref):
    total = weighted(high_ref, low_ref, 0, rows_ref).astype(BF)
    half = top_ref.shape[0]
    top_ref[...], bottom_ref[...] = total[:half], total[half:]


def add_kernel(high_ref, low_ref, rows_ref, top_ref, bottom_ref, below_ref, above_ref):
    half = top_ref.shape[0]
    below = weighted(high_ref, low_ref, 0, rows_ref)
    above = weighted(high_ref, low_ref, 1, rows_ref)
    below_ref[:half, :] = (below[:half] + top_ref[...].astype(F32)).astype(BF)
    below_ref[half:, :] = below[half:].astype(BF)
    above_ref[:half, :] = above[:half].astype(BF)
    above_ref[half:, :] = (above[half:] + bottom_ref[...].astype(F32)).astype(BF)


def last_kernel(high_ref, low_ref, rows_ref, *refs):
    left, right, out_ref = refs[0:2], refs[2:4], refs[4]
    total = weighted(high_ref, low_ref, 0, rows_ref)
    first = pl.program_id(0) < pl.num_programs(0) // 2

    @pl.when(first)
    def _():
        out_ref[...] = (total + left[0][...].astype(F32) + left[1][...].astype(F32)).astype(BF)

    @pl.when(jnp.logical_not(first))
    def _():
        out_ref[...] = (total + right[0][...].astype(F32) + right[1][...].astype(F32)).astype(BF)


def combine(kernel, plans, rows, first, steps, more, counts):
    _, high, low = plans
    table = pl.BlockSpec(high.shape, lambda j: (0, 0, 0))
    return pl.pallas_call(
        kernel,
        grid=(steps,),
        out_shape=[jax.ShapeDtypeStruct((n, steps * TILE), BF) for n in counts],
        in_specs=[
            table,
            table,
            pl.BlockSpec(rows.shape[:-1] + (TILE,), lambda j: (0, 0, 0, first + j)),
        ]
        + [pl.BlockSpec(a.shape, lambda j: (0, 0)) for a in more],
        out_specs=[pl.BlockSpec((n, TILE), lambda j: (0, j)) for n in counts],
        compiler_params=PARAMS,
        name="combine",
    )(high, low, rows, *more)


def over_y(rows, shape):
    return lax.all_to_all(
        rows.reshape(YS, -1, rows.shape[-1]), "y", split_axis=0, concat_axis=0, tiled=True
    ).reshape(shape)


def on_device(tokens, route_ids, gate_values, w_gate_up, w_down):
    tok_rows, top = route_ids.shape
    model = tokens.shape[1]
    slots = 3 * tok_rows * top // (2 * ZH * YS)
    half = tok_rows // 2
    swap = [(0, 1), (1, 0)]
    group = lax.axis_index("zh").reshape(1)
    barrier = lax.optimization_barrier
    pack = pack_shards(w_gate_up[0], w_down[0])
    meta = jnp.concatenate([route_ids.astype(F32).T, gate_values.T], axis=0)

    near = [lax.ppermute(tokens, "zh", ring(k)) for k in (1, 3)]
    near_metas = [lax.ppermute(meta, "zh", ring(k)) for k in (1, 3)]
    swapped = lax.ppermute(pack, "zl", swap)
    mine = lax.all_gather(pack, "x")
    own = plan(group, slots, meta)
    arrived_own = over_y(gather(own[0], tokens), (-1, model))
    near, near_metas, swapped, arrived_own = barrier((near, near_metas, swapped, arrived_own))
    other = lax.all_gather(swapped, "x")

    sides = plan(group, slots, *near_metas)
    arrived_sides = over_y(gather(sides[0], *near), (-1, model))
    far = [lax.ppermute(near[0][:half], "zh", ring(1)), lax.ppermute(near[1][half:], "zh", ring(3))]
    far_meta = lax.ppermute(near_metas[0], "zh", ring(1))
    across = plan(group, slots, far_meta)
    sent, mine, arrived_sides = barrier((gather(across[0], *far), mine, arrived_sides))
    mine_swapped = lax.ppermute(mine, "core", swap)
    arrived_across = over_y(sent, (-1, model))
    packs = [mine, mine_swapped, other, lax.ppermute(other, "core", swap)]
    zl, core = lax.axis_index("zl"), lax.axis_index("core")
    place = jnp.stack([zl * 2 + core, zl * 2 + 1 - core, (1 - zl) * 2 + core, (1 - zl) * 2 + 1 - core])

    made_sides = expert(place, arrived_sides, packs, 2)
    made_sides, arrived_across = barrier((made_sides, arrived_across))
    (made,) = expert(place, arrived_across, packs, 1)

    back = over_y(made, (YS, 1, slots, model))
    pieces = range(model // TILE)
    parts = [combine(split_kernel, across, back, p, 1, [], (half, half)) for p in pieces]
    passed = [
        [lax.ppermute(top, "zh", ring(3)), lax.ppermute(bottom, "zh", ring(1))] for top, bottom in parts
    ]
    arrived_own, parts = barrier((arrived_own, parts))
    (made_own,) = expert(place, arrived_own, packs, 1)
    home, rows = [], made_sides[0]
    for p in pieces:
        rows, back = barrier((rows, back))
        back = over_y(rows, (YS, 2, slots, TILE))
        if p == 0:
            rows, passed[0], made_own = barrier((made_sides[1], passed[0], made_own))
            back, passed[1] = barrier((back, passed[1]))
        below, above = combine(add_kernel, sides, back, 0, 1, passed[p], (tok_rows, tok_rows))
        if p == 1:
            made_own, home, below, above = barrier((made_own, home, below, above))
        home = home + [lax.ppermute(below, "zh", ring(3)), lax.ppermute(above, "zh", ring(1))]
    back = over_y(made_own, (YS, 1, slots, model))
    return combine(last_kernel, own, back, 0, len(pieces), home, (tok_rows,))[0]


def solution(mesh):
    split = Mesh(mesh.devices.reshape(ZH, YS, XS, 2, 2), ("zh", "y", "x", "zl", "core"))
    owner, shard = ("zh", "y"), ("x", "zl", "core")
    every = owner + shard
    in_specs = (P(every, None),) * 3 + (P(owner, shard, None), P(owner, None, shard))
    return jax.shard_map(
        on_device, mesh=split, in_specs=in_specs, out_specs=P(every, None), check_vma=False
    )
```
